32 devices in a mesh: atm: 8 (over y, x, core), xg: 4 (over z).
Axes of the slice: x: 2, y: 2, z: 4, core: 2. Of those that a mesh axis runs over, the one named last changes fastest.
Arguments:
- fields_now: float32 [128, 48, 52, 128], P('atm', None, 'xg'), may hold values from -6 to 6
- upper: float32 [128, 48, 128], P(('atm', 'xg')), may hold values from 0.05 to 20
- lower: float32 [128, 48, 128], P(('atm', 'xg')), may hold values from 0.05 to 20
- surface_gain: float32 [128, 128], P(('atm', 'xg')), may hold values from 0.3 to 3
- route: int32 [8, 32, 2], P('atm'), may hold values from 0 to 16
- margin_slot: int32 [32, 96], P(('atm', 'xg')), may hold values from 0 to 15
- margin_block: int32 [32, 96], P(('atm', 'xg')), may hold values from 0 to 15
- margin_count: int32 [32], P(('atm', 'xg')), may hold values from 12 to 96, as said below
- margin_weight: float32 [32, 96, 128, 128], P(('atm', 'xg')), may hold values from 0 to 0.03
- surface_value: float32 [512, 52, 128], P(('atm', 'xg')), may hold values from -6 to 6
- exchange_coef: float32 [512, 128], P(('atm', 'xg')), may hold values from 0.05 to 2
- land_mask: int32 [512, 128], P(('atm', 'xg')), may hold values 0 or 1
- land_gain: float32 [512, 128], P(('atm', 'xg')), may hold values from 0.2 to 5
Outputs:
- fields_next: float32 [128, 48, 52, 128], P('atm', None, 'xg')
- surface_flux: float32 [512, 52, 128], P(('atm', 'xg'))
The draws below stay inside these ranges and needn't reach their ends.
Inputs may be any that keep to these rules, and one draw needn't show every extreme that they name: `route`: the value 16 marks an empty slot; other values name a local column block of the sending atmosphere index. `margin_slot`: A value s names slot s % 2 from atmosphere index s // 2. `margin_count`: margins from this count on are padding; some owner has all 96 live.
All inputs are finite; a program needn't handle non-finite values. No bound on the sum of `land_mask` on one device may be relied on, other than what follows from the above.
Results may differ from the reference program's by a relative error of at most 0.0003.
Values sent between devices are 32-bit elements; how exact they have to be, the bound alone decides.
No kernel may reach another device: no remote copies, remote signals or barrier semaphores. Data moves between devices by JAX's collectives and lax.ppermute only.
A program may use at most 128 MiB of HBM per device.

```python
import math
import jax
import jax.numpy as jnp
from jax import lax

BLOCK = 128
LEVELS = 48
FIELDS = 52
ATM_BLOCKS = 16
XG_BLOCKS = 16
PAIR_SLOTS = 2
MARGINS = 96
OWNERS = 32
COLUMN_BLOCKS = 128
CELL_BLOCKS = 512
N_ATM = 8


def draw_margin_count(key, part):
    first, second = jax.random.split(jax.random.fold_in(key, 17))
    counts = jax.random.randint(first, (OWNERS,), MARGINS // 8, MARGINS // 2 + 1)
    fullest = jax.random.randint(second, (), 0, OWNERS)
    return jnp.where(jnp.arange(OWNERS) == fullest, MARGINS, counts).astype(jnp.int32)


def plant(entries, rng, least, largest):
    spot = [jax.random.randint(jax.random.fold_in(rng, axis), (), 0, length) for axis, length in enumerate(entries.shape)]
    main_axis = entries.shape.index(max(entries.shape))
    next_to = spot[:main_axis] + [(spot[main_axis] + 1) % entries.shape[main_axis]] + spot[main_axis + 1:]
    return entries.at[tuple(spot)].set(least).at[tuple(next_to)].set(largest)


def levels(stream_key, dims, cuts, least, largest):
    factor_of, own = 1.0, jax.random.fold_in(stream_key, 6)
    for axis_at, blocks in cuts:
        draws = jnp.exp(jax.random.uniform(jax.random.fold_in(own, axis_at), (blocks,), jnp.float32, least / len(cuts), largest / len(cuts)))
        factor_of = factor_of * jnp.repeat(draws, dims[axis_at] // blocks).reshape([-1 if axis == axis_at else 1 for axis in range(len(dims))])
    return factor_of


def centred(rng, shape, scale, most, cuts=(), held_as=jnp.bfloat16):
    gain = levels(rng, shape, cuts, -0.22, 0.18) if cuts else 1.0
    result = jax.random.normal(rng, shape, jnp.float32) * scale * gain
    return jnp.minimum(jnp.maximum(result, -most), most).astype(held_as)


def setup_inputs(seed: int = 0) -> dict:
    keys = jax.random.split(jax.random.key(seed), 14)
    fields_now = centred(keys[0], (COLUMN_BLOCKS, LEVELS, FIELDS, BLOCK), 1.0, 6.0, ((0, 8), (2, 4)), jnp.float32)
    upper = jnp.clip(jnp.exp(math.log(20.0) - 5.9914645 * jax.random.uniform(keys[1], (COLUMN_BLOCKS, LEVELS, BLOCK), jnp.float32) ** levels(keys[1], (COLUMN_BLOCKS, LEVELS, BLOCK), ((0, 32),), -0.2, 0.2)), 0.05, 20.0)
    lower = jnp.clip(jnp.exp(math.log(20.0) - 5.9914645 * jax.random.uniform(keys[2], (COLUMN_BLOCKS, LEVELS, BLOCK), jnp.float32) ** levels(keys[2], (COLUMN_BLOCKS, LEVELS, BLOCK), ((0, 32),), -0.2, 0.2)), 0.05, 20.0)
    surface_gain = jnp.clip(jnp.exp(math.log(3.0) - 2.3025851 * jax.random.uniform(keys[3], (COLUMN_BLOCKS, BLOCK), jnp.float32) ** levels(keys[3], (COLUMN_BLOCKS, BLOCK), ((0, 32),), -0.2, 0.2)), 0.3, 3.0)
    route = plant(jax.random.randint(keys[4], (N_ATM, OWNERS, PAIR_SLOTS), 0, ATM_BLOCKS + 1), jax.random.fold_in(keys[4], 1), 0, ATM_BLOCKS).astype(jnp.int32)
    margin_slot = plant(jax.random.randint(keys[5], (OWNERS, MARGINS), 0, N_ATM * PAIR_SLOTS), jax.random.fold_in(keys[5], 1), 0, (N_ATM * PAIR_SLOTS) - 1).astype(jnp.int32)
    margin_block = plant(jax.random.randint(keys[6], (OWNERS, MARGINS), 0, XG_BLOCKS), jax.random.fold_in(keys[6], 1), 0, XG_BLOCKS - 1).astype(jnp.int32)
    margin_count = draw_margin_count(jax.random.fold_in(keys[13], 71), 0)
    margin_weight = jnp.clip(0.03 * jax.random.uniform(keys[8], (OWNERS, MARGINS, BLOCK, BLOCK), jnp.float32) ** levels(keys[8], (OWNERS, MARGINS, BLOCK, BLOCK), ((0, 32),), -0.2, 0.2), 0.0, 0.03)
    surface_value = centred(keys[9], (CELL_BLOCKS, FIELDS, BLOCK), 1.0, 6.0, ((0, 32),), jnp.float32)
    exchange_coef = jnp.clip(jnp.exp(math.log(2.0) - 3.6888794 * jax.random.uniform(keys[10], (CELL_BLOCKS, BLOCK), jnp.float32) ** levels(keys[10], (CELL_BLOCKS, BLOCK), ((0, 32),), -0.2, 0.2)), 0.05, 2.0)
    land_mask = plant((jax.random.randint(keys[11], (CELL_BLOCKS, BLOCK), 0, 3) < 1).astype(jnp.int32), jax.random.fold_in(keys[11], 1), 0, 1)
    land_gain = jnp.clip(jnp.exp(math.log(5.0) - 3.218876 * jax.random.uniform(keys[12], (CELL_BLOCKS, BLOCK), jnp.float32) ** levels(keys[12], (CELL_BLOCKS, BLOCK), ((0, 32),), -0.2, 0.2)), 0.2, 5.0)
    return {"fields_now": fields_now, "upper": upper, "lower": lower, "surface_gain": surface_gain, "route": route, "margin_slot": margin_slot, "margin_block": margin_block, "margin_count": margin_count, "margin_weight": margin_weight, "surface_value": surface_value, "exchange_coef": exchange_coef, "land_mask": land_mask, "land_gain": land_gain}


HIGHEST = lax.Precision.HIGHEST


def factors(upper, lower):
    level_count = upper.shape[1]
    carried = jnp.zeros_like(upper[:, 0])
    inverses, multipliers, carries = [], [], []
    for height in range(level_count):
        from_above = upper[:, height] if height > 0 else jnp.zeros_like(carried)
        from_below = lower[:, height] if height < level_count - 1 else jnp.zeros_like(carried)
        inverse = 1.0 / (1.0 + from_above + from_below - from_above * carried)
        carried = from_below * inverse
        inverses.append(inverse)
        multipliers.append(from_above * inverse)
        carries.append(carried)
    return jnp.stack(inverses, 1), jnp.stack(multipliers, 1), jnp.stack(carries, 1)


def reference(fields_now, upper, lower, surface_gain, route, margin_slot, margin_block, margin_count, margin_weight, surface_value, exchange_coef, land_mask, land_gain):
    inverse, multiplier, carry_factor = factors(upper, lower)
    bottom_gain = surface_gain * inverse[:, -1]
    running = jnp.zeros_like(fields_now[:, 0])
    partials = []
    for height in range(LEVELS):
        running = inverse[:, height, None, :] * fields_now[:, height] + multiplier[:, height, None, :] * running
        partials.append(running)
    padded_value = jnp.concatenate([running, jnp.zeros((1, FIELDS, BLOCK), jnp.float32)], 0)
    padded_gain = jnp.concatenate([bottom_gain, jnp.zeros((1, BLOCK), jnp.float32)], 0)
    land_total = land_mask.astype(jnp.float32) * land_gain

    def owner_step(flux_total, owner):
        slot_index = margin_slot[owner]
        source = slot_index // PAIR_SLOTS
        pair_index = slot_index % PAIR_SLOTS
        local_block = route[source, owner, pair_index]
        alive = (jnp.arange(MARGINS, dtype=jnp.int32) < margin_count[owner]) & (local_block < ATM_BLOCKS)
        global_block = jnp.where(alive, source * ATM_BLOCKS + local_block, COLUMN_BLOCKS).astype(jnp.int32)
        alive_float = alive.astype(jnp.float32)
        weight = margin_weight[owner]
        value_part = jnp.einsum("kxb,kfb->kfx", weight, padded_value[global_block], precision=HIGHEST)
        gain_part = jnp.einsum("kxb,kb->kx", weight, padded_gain[global_block], precision=HIGHEST)
        select = (margin_block[owner][None, :] == jnp.arange(XG_BLOCKS, dtype=jnp.int32)[:, None]).astype(jnp.float32) * alive_float[None, :]
        cell_value = jnp.einsum("jk,kfx->jfx", select, value_part, precision=HIGHEST)
        cell_gain = jnp.einsum("jk,kx->jx", select, gain_part, precision=HIGHEST)
        start = (owner * XG_BLOCKS).astype(jnp.int32)
        own_surface = lax.dynamic_slice_in_dim(surface_value, start, XG_BLOCKS, 0)
        own_coef = lax.dynamic_slice_in_dim(exchange_coef, start, XG_BLOCKS, 0)[:, None, :]
        own_land = lax.dynamic_slice_in_dim(land_total, start, XG_BLOCKS, 0)
        cell_flux = own_coef * (own_surface - cell_value) / (1.0 + own_coef * (cell_gain + own_land)[:, None, :])
        returned = jnp.einsum("kxb,kfx->kfb", weight, cell_flux[margin_block[owner]], precision=HIGHEST)
        returned = returned * alive_float[:, None, None]
        flux_total = flux_total.at[global_block].add(returned)
        return flux_total, cell_flux

    start_total = jnp.zeros((COLUMN_BLOCKS + 1, FIELDS, BLOCK), jnp.float32)
    flux_total, fluxes = lax.scan(owner_step, start_total, jnp.arange(OWNERS, dtype=jnp.int32))
    surface_flux = fluxes.reshape(CELL_BLOCKS, FIELDS, BLOCK)
    column_flux = flux_total[:COLUMN_BLOCKS]
    state = running + bottom_gain[:, None, :] * column_flux
    outputs = [state]
    for height in range(LEVELS - 2, -1, -1):
        state = partials[height] + carry_factor[:, height, None, :] * state
        outputs.append(state)
    fields_next = jnp.stack(outputs[::-1], 1)
    return fields_next, surface_flux
```

```python
import functools
import math

import jax
import jax.numpy as jnp
from jax import lax
from jax.experimental import pallas as pl
from jax.experimental.pallas import tpu as pltpu
from jax.sharding import PartitionSpec as P

F32 = jnp.float32
BF16 = jnp.bfloat16
ROWS = 8


def vmem():
    return pl.BlockSpec(memory_space=pltpu.VMEM)


def smem():
    return pl.BlockSpec(memory_space=pltpu.SMEM)


def hbm():
    return pl.BlockSpec(memory_space=pl.ANY)


def params(limit=None):
    return pltpu.CompilerParams(vmem_limit_bytes=limit)


def round_up(value, step):
    return -(-value // step) * step


def split(value):
    high = value.astype(BF16)
    low = (value - high.astype(F32)).astype(BF16)
    return high, low


def factor_kernel(levels, own, upper_ref, lower_ref, gain_ref, first_ref, second_ref, inverse_ref):
    carried = jnp.zeros(gain_ref.shape, F32)
    for k in range(levels):
        from_above = upper_ref[pl.ds(k, own, stride=levels), :] if k > 0 else jnp.zeros_like(carried)
        from_below = lower_ref[pl.ds(k, own, stride=levels), :] if k < levels - 1 else jnp.zeros_like(carried)
        inverse = 1.0 / (1.0 + from_above + from_below - from_above * carried)
        carried = from_below * inverse
        inverse_ref[k] = inverse
        second_ref[k] = from_above * inverse
        second_ref[levels + k] = carried
    product = inverse_ref[levels - 1]
    first_ref[levels] = gain_ref[...] * product
    first_ref[levels - 1] = product
    product = second_ref[levels - 1]
    for k in range(levels - 2, -1, -1):
        first_ref[k] = inverse_ref[k] * product
        product = product * second_ref[k]


def factors(upper, lower, surface_gain):
    own, levels, width = upper.shape
    return pl.pallas_call(
        functools.partial(factor_kernel, levels, own),
        out_shape=(
            jax.ShapeDtypeStruct((levels + 1, own, width), F32),
            jax.ShapeDtypeStruct((2 * levels, own, width), F32),
        ),
        in_specs=[vmem()] * 3,
        out_specs=(vmem(), vmem()),
        scratch_shapes=[pltpu.VMEM((levels, own, width), F32)],
        compiler_params=params(8 << 20),
        cost_estimate=pl.CostEstimate(flops=1000000, bytes_accessed=400000, transcendentals=30000),
        name="factors",
    )(upper.reshape(own * levels, width), lower.reshape(own * levels, width), surface_gain)


def fetch_fields(me, groups, own, fields_ref, held_ref, sem):
    shares = fields_ref.shape[1]
    for f in range(shares):
        for q in range(groups):
            base = lax.rem(me - q + groups, groups) * own
            for i in range(own):
                pltpu.make_async_copy(
                    fields_ref.at[base + i, f], held_ref.at[f, :, q * own + i, :], sem.at[f]
                ).start()


def bottom_kernel(groups, own, rows, me_ref, place_ref, *refs):
    parts, fields_ref, send_ref, held_ref, weight_ref, value_ref, sem = (
        refs[:groups], *refs[groups:]
    )
    fetch_fields(me_ref[0], groups, own, fields_ref, held_ref, sem)
    blocks = groups * own
    levels = held_ref.shape[1]
    shares = held_ref.shape[0]
    for q in range(groups):
        weight_ref[:, q * own:(q + 1) * own, :] = parts[q][...]
    value_ref[...] = jnp.zeros_like(value_ref)
    value_ref[pl.ds(shares, blocks, stride=rows), :] = weight_ref[levels]
    for f in range(shares):
        pltpu.make_async_copy(held_ref.at[f], held_ref.at[f], sem.at[f]).wait()
        sums = [None] * 4
        for k in range(levels):
            term = weight_ref[k] * held_ref[f, k]
            sums[k % 4] = term if sums[k % 4] is None else sums[k % 4] + term
        value_ref[pl.ds(f, blocks, stride=rows), :] = (sums[0] + sums[1]) + (sums[2] + sums[3])
    owners, slot_rows = send_ref.shape[:2]
    slots = slot_rows // rows
    for d in range(owners):
        for p in range(slots):
            start = pl.multiple_of(place_ref[d * slots + p] * rows, rows)
            send_ref[d, p * rows:(p + 1) * rows, :] = value_ref[pl.ds(start, rows), :]


def bottoms(me, place, parts, fields, owners, slots, rows):
    blocks, shares, levels, width = fields.shape
    groups = len(parts)
    own = blocks // groups
    return pl.pallas_call(
        functools.partial(bottom_kernel, groups, own, rows),
        out_shape=jax.ShapeDtypeStruct((owners, slots * rows, width), F32),
        in_specs=[smem(), smem()] + [vmem()] * groups + [hbm()],
        out_specs=vmem(),
        scratch_shapes=[
            pltpu.VMEM((shares, levels, blocks, width), F32),
            pltpu.VMEM((levels + 1, blocks, width), F32),
            pltpu.VMEM(((blocks + 1) * rows, width), F32),
            pltpu.SemaphoreType.DMA((shares,)),
        ],
        compiler_params=params(16 << 20),
        cost_estimate=pl.CostEstimate(flops=4000000, bytes_accessed=7000000, transcendentals=0),
        name="bottoms",
    )(me, place, *parts, fields)


def split_kernel(weight_ref, out_ref):
    high, low = split(weight_ref[...])
    size = weight_ref.shape[1]
    out_ref[:, :size, :] = high
    out_ref[:, size:, :] = low


def split_weights(weight, step=8):
    margins, cells, columns = weight.shape
    step = math.gcd(step, margins)
    return pl.pallas_call(
        split_kernel,
        grid=(margins // step,),
        out_shape=jax.ShapeDtypeStruct((margins, 2 * cells, columns), BF16),
        in_specs=[pl.BlockSpec((step, cells, columns), lambda i: (i, 0, 0))],
        out_specs=pl.BlockSpec((step, 2 * cells, columns), lambda i: (i, 0, 0)),
        compiler_params=params(8 << 20),
        cost_estimate=pl.CostEstimate(flops=5000000, bytes_accessed=13000000, transcendentals=0),
        name="split_weights",
    )(weight)


def margin_kernel(
    groups, rows, slots, gain_row, unroll,
    slot_ref, block_ref, count_ref, weight_hbm, got_ref, surface_ref, coef_ref, mask_ref, land_ref,
    reply_ref, flux_ref,
    weight_ref, value_ref, cell_ref, two_ref, back_ref, sem,
):
    margins = weight_ref.shape[0]
    chunks = sem.shape[0]
    size = margins // chunks
    for c in range(chunks):
        pltpu.make_async_copy(
            weight_hbm.at[pl.ds(c * size, size)], weight_ref.at[pl.ds(c * size, size)], sem.at[c]
        ).start()
    tall = groups * rows
    columns = weight_ref.shape[2]
    sources = value_ref.shape[0] // slots
    cells = surface_ref.shape[0]
    count = count_ref[0]
    for a in range(sources):
        for p in range(slots):
            for g in range(groups):
                high, low = split(got_ref[a * groups + g, p * rows:(p + 1) * rows, :])
                value_ref[a * slots + p, g * rows:(g + 1) * rows, :] = high
                value_ref[a * slots + p, tall + g * rows:tall + (g + 1) * rows, :] = low
    cell_ref[...] = jnp.zeros_like(cell_ref)
    back_ref[...] = jnp.zeros_like(back_ref)

    for c in range(chunks):
        pltpu.make_async_copy(
            weight_hbm.at[pl.ds(c * size, size)], weight_ref.at[pl.ds(c * size, size)], sem.at[c]
        ).wait()

        @pl.loop(0, size // unroll)
        def _(step):
            for u in range(unroll):
                k = c * size + step * unroll + u
                target = jnp.where(k < count, block_ref[k], cells)
                product = lax.dot_general(
                    value_ref[slot_ref[k]], weight_ref[k], (((1,), (1,)), ((), ())),
                    preferred_element_type=F32,
                )
                cell_ref[target] += (
                    product[:tall, :columns] + (product[tall:, :columns] + product[:tall, columns:])
                )

    for j in range(cells):
        cell = cell_ref[j]
        coef = coef_ref[j:j + 1, :]
        land = mask_ref[j:j + 1, :].astype(F32) * land_ref[j:j + 1, :]
        scale = coef / (1.0 + coef * (cell[gain_row:gain_row + 1, :] + land))
        flux = scale * (surface_ref[j] - cell)
        flux_ref[j] = flux
        high, low = split(flux)
        two_ref[j, :tall, :columns] = high
        two_ref[j, :tall, columns:] = high
        two_ref[j, tall:, :columns] = low
        two_ref[j, tall:, columns:] = low

    @pl.loop(0, margins // unroll)
    def _(step):
        for u in range(unroll):
            k = step * unroll + u
            target = jnp.where(k < count, slot_ref[k], sources * slots)
            product = lax.dot_general(
                two_ref[block_ref[k]], weight_ref[k], (((1,), (0,)), ((), ())),
                preferred_element_type=F32,
            )
            back_ref[target] += product[:tall] + product[tall:]

    for a in range(sources):
        for p in range(slots):
            for g in range(groups):
                reply_ref[a * groups + g, p * rows:(p + 1) * rows, :] = (
                    back_ref[a * slots + p, g * rows:(g + 1) * rows, :]
                )


def margins_stage(slot, block, count, weights, got, surface, coef, mask, land, groups, rows, slots, gain_row):
    margins, twice, columns = weights.shape
    owners, slot_rows, width = got.shape
    cells, tall, _ = surface.shape
    sources = owners // groups
    unroll = 4
    chunks = 6
    return pl.pallas_call(
        functools.partial(margin_kernel, groups, rows, slots, gain_row, unroll),
        out_shape=(
            jax.ShapeDtypeStruct(got.shape, F32),
            jax.ShapeDtypeStruct(surface.shape, F32),
        ),
        in_specs=[smem()] * 3 + [hbm()] + [vmem()] * 5,
        out_specs=(vmem(), vmem()),
        scratch_shapes=[
            pltpu.VMEM(weights.shape, BF16),
            pltpu.VMEM((sources * slots, 2 * tall, width), BF16),
            pltpu.VMEM((cells + 1, tall, width), F32),
            pltpu.VMEM((cells, 2 * tall, 2 * width), BF16),
            pltpu.VMEM((sources * slots + 1, tall, width), F32),
            pltpu.SemaphoreType.DMA((chunks,)),
        ],
        compiler_params=params(24 << 20),
        cost_estimate=pl.CostEstimate(flops=800000000, bytes_accessed=8000000, transcendentals=0),
        name="margins",
    )(slot, block, count, weights, got, surface, coef, mask, land)


def sweep_kernel(groups, own, me_ref, *refs):
    parts, gains, fields_ref, after_ref, still_ref, reach_ref, held_ref, factor_ref, sem, out_sem = (
        refs[:groups], refs[groups:2 * groups], *refs[2 * groups:]
    )
    fetch_fields(me_ref[0], groups, own, fields_ref, held_ref, sem)
    shares, levels, blocks, width = held_ref.shape
    for q in range(groups):
        factor_ref[levels:, q * own:(q + 1) * own, :] = parts[q][...]
        reach_ref[levels - 1, q * own:(q + 1) * own, :] = gains[q][levels]
    reach = reach_ref[levels - 1]
    for k in range(levels - 1, -1, -1):
        carry = factor_ref[2 * levels + k]
        above = factor_ref[2 * levels + k - 1] if k > 0 else jnp.zeros_like(carry)
        factor_ref[k] = 1.0 - carry - factor_ref[levels + k] * (1.0 - above)
        if k < levels - 1:
            reach = carry * reach
            reach_ref[k] = reach
    for f in range(shares):
        pltpu.make_async_copy(held_ref.at[f], held_ref.at[f], sem.at[f]).wait()
        partial = factor_ref[0] * held_ref[f, 0]
        held_ref[f, 0] = partial
        for k in range(1, levels):
            partial = factor_ref[k] * held_ref[f, k] + factor_ref[levels + k] * partial
            held_ref[f, k] = partial
        for k in range(levels - 2, -1, -1):
            partial = held_ref[f, k] + factor_ref[2 * levels + k] * partial
            held_ref[f, k] = partial
        pltpu.make_async_copy(held_ref.at[f], still_ref.at[f], out_sem.at[f]).start()
    for f in range(shares):
        pltpu.make_async_copy(held_ref.at[f], still_ref.at[f], out_sem.at[f]).wait()


def sweeps(me, parts, gains, fields, after):
    blocks, shares, levels, width = fields.shape
    groups = len(parts)
    own = blocks // groups
    return pl.pallas_call(
        functools.partial(sweep_kernel, groups, own),
        out_shape=(
            jax.ShapeDtypeStruct((shares, levels, blocks, width), F32),
            jax.ShapeDtypeStruct((levels, blocks, width), F32),
        ),
        in_specs=[smem()] + [vmem()] * (2 * groups) + [hbm(), hbm()],
        out_specs=(hbm(), vmem()),
        scratch_shapes=[
            pltpu.VMEM((shares, levels, blocks, width), F32),
            pltpu.VMEM((3 * levels, blocks, width), F32),
            pltpu.SemaphoreType.DMA((shares,)),
            pltpu.SemaphoreType.DMA((shares,)),
        ],
        compiler_params=params(16 << 20),
        cost_estimate=pl.CostEstimate(flops=8000000, bytes_accessed=12000000, transcendentals=0),
        name="sweeps",
    )(me, *parts, *gains, fields, after)


def finish_kernel(groups, own, rows, me_ref, place_ref, answer_ref, still_ref, reach_ref, out_ref,
                  held_ref, flux_ref, sem, out_sem):
    shares, levels, blocks, width = held_ref.shape
    for f in range(shares):
        pltpu.make_async_copy(still_ref.at[f], held_ref.at[f], sem.at[f]).start()
    flux_ref[...] = jnp.zeros_like(flux_ref)
    owners, slot_rows = answer_ref.shape[:2]
    slots = slot_rows // rows
    for d in range(owners):
        for p in range(slots):
            start = pl.multiple_of(place_ref[d * slots + p] * rows, rows)
            flux_ref[pl.ds(start, rows), :] += answer_ref[d, p * rows:(p + 1) * rows, :]
    me = me_ref[0]
    copies = []
    for f in range(shares):
        flux = flux_ref[pl.ds(f, blocks, stride=rows), :]
        pltpu.make_async_copy(still_ref.at[f], held_ref.at[f], sem.at[f]).wait()
        for k in range(levels):
            held_ref[f, k] = held_ref[f, k] + reach_ref[k] * flux
        for q in range(groups):
            base = lax.rem(me - q + groups, groups) * own
            for i in range(own):
                pltpu.make_async_copy(
                    held_ref.at[f, :, q * own + i, :], out_ref.at[base + i, f], out_sem.at[f]
                ).start()
    for f in range(shares):
        pltpu.make_async_copy(held_ref.at[f], held_ref.at[f], out_sem.at[f]).wait()


def finish(me, place, answer, still, reach, groups, rows):
    shares, levels, blocks, width = still.shape
    return pl.pallas_call(
        functools.partial(finish_kernel, groups, blocks // groups, rows),
        out_shape=jax.ShapeDtypeStruct((blocks, shares, levels, width), F32),
        in_specs=[smem(), smem(), vmem(), hbm(), vmem()],
        out_specs=hbm(),
        scratch_shapes=[
            pltpu.VMEM((shares, levels, blocks, width), F32),
            pltpu.VMEM(((blocks + 1) * rows, width), F32),
            pltpu.SemaphoreType.DMA((shares,)),
            pltpu.SemaphoreType.DMA((shares,)),
        ],
        compiler_params=params(16 << 20),
        cost_estimate=pl.CostEstimate(flops=4000000, bytes_accessed=12000000, transcendentals=0),
        name="finish",
    )(me, place, answer, still, reach)


def per_device(
    fields_now, upper, lower, surface_gain, route, margin_slot, margin_block, margin_count,
    margin_weight, surface_value, exchange_coef, land_mask, land_gain,
):
    groups = lax.axis_size("xg")
    me = lax.axis_index("xg").astype(jnp.int32)
    blocks, levels, shares, width = fields_now.shape
    own = blocks // groups
    rows = round_up(shares + 1, ROWS)
    owners, slots = route.shape[1:]
    cells = surface_value.shape[0]

    def shift(array, by):
        return lax.ppermute(array, "xg", [(i, (i + by) % groups) for i in range(groups)])

    def shared(array):
        return [array] + [shift(array, by) for by in range(1, groups)]

    fields = fields_now.transpose(0, 2, 1, 3)
    first, second = factors(upper, lower, surface_gain)
    firsts = shared(first)
    routing = route[0].reshape(owners * slots)
    place = jnp.where(
        routing < blocks,
        lax.rem(me - routing // own + groups, groups) * own + routing % own,
        blocks,
    ).astype(jnp.int32)
    me = me[None]
    weights = split_weights(margin_weight[0])
    surface = jnp.pad(
        surface_value.reshape(cells, groups, shares, width),
        ((0, 0), (0, 0), (0, rows - shares), (0, 0)),
    ).reshape(cells, groups * rows, width)
    send = bottoms(me, place, firsts, fields, owners, slots, rows)
    second, send = lax.optimization_barrier((second, send))
    got = lax.all_to_all(send, ("atm", "xg"), split_axis=0, concat_axis=0, tiled=True)
    seconds = shared(second)
    reply, flux = margins_stage(
        margin_slot[0], margin_block[0], margin_count, weights, got, surface,
        exchange_coef, land_mask, land_gain, groups, rows, slots, shares,
    )
    answer = lax.all_to_all(reply, ("atm", "xg"), split_axis=0, concat_axis=0, tiled=True)
    still, reach = sweeps(me, seconds, firsts, fields, reply)
    surface_flux = flux.reshape(cells, groups, rows, width)[:, :, :shares].reshape(
        cells, groups * shares, width
    )
    out = finish(me, place, answer, still, reach, groups, rows)
    return out.transpose(0, 2, 1, 3), surface_flux


def solution(mesh):
    in_specs = (
        P("atm", None, "xg", None),
        P(("atm", "xg"), None, None),
        P(("atm", "xg"), None, None),
        P(("atm", "xg"), None),
        P("atm", None, None),
        P(("atm", "xg"), None),
        P(("atm", "xg"), None),
        P(("atm", "xg")),
        P(("atm", "xg"), None, None, None),
        P(("atm", "xg"), None, None),
        P(("atm", "xg"), None),
        P(("atm", "xg"), None),
        P(("atm", "xg"), None),
    )
    out_specs = (P("atm", None, "xg", None), P(("atm", "xg"), None, None))
    return jax.shard_map(
        per_device, mesh=mesh, in_specs=in_specs, out_specs=out_specs, check_vma=False
    )
```

```python
import functools
import math

import jax
import jax.numpy as jnp
from jax import lax
from jax.experimental import pallas as pl
from jax.experimental.pallas import tpu as pltpu
from jax.sharding import PartitionSpec as P

F32 = jnp.float32
BF16 = jnp.bfloat16
ROWS = 8
MOST = 67043328
ROOMY = 50 << 20


def vmem():
    return pl.BlockSpec(memory_space=pltpu.VMEM)


def smem():
    return pl.BlockSpec(memory_space=pltpu.SMEM)


def hbm():
    return pl.BlockSpec(memory_space=pltpu.HBM)


def params(limit):
    return pltpu.CompilerParams(vmem_limit_bytes=limit)


def round_up(value, step):
    return -(-value // step) * step


def split(value):
    high = value.astype(BF16)
    low = (value - high.astype(F32)).astype(BF16)
    return high, low


def factor_kernel(levels, own, upper_hbm, lower_hbm, gain_hbm, first_ref, second_ref,
                  upper_ref, lower_ref, gain_ref, inverse_ref, sem):
    copies = [
        pltpu.make_async_copy(source, target, sem.at[i])
        for i, (source, target) in enumerate(
            ((upper_hbm, upper_ref), (lower_hbm, lower_ref), (gain_hbm, gain_ref))
        )
    ]
    for copy in copies:
        copy.start()
    for copy in copies:
        copy.wait()
    carried = jnp.zeros(gain_ref.shape, F32)
    for k in range(levels):
        from_above = upper_ref[pl.ds(k, own, stride=levels), :] if k > 0 else jnp.zeros_like(carried)
        from_below = lower_ref[pl.ds(k, own, stride=levels), :] if k < levels - 1 else jnp.zeros_like(carried)
        inverse = 1.0 / (1.0 + from_above + from_below - from_above * carried)
        carried = from_below * inverse
        inverse_ref[k] = inverse
        second_ref[k] = from_above * inverse
        second_ref[levels + k] = carried
    product = inverse_ref[levels - 1]
    first_ref[levels] = gain_ref[...] * product
    first_ref[levels - 1] = product
    product = second_ref[levels - 1]
    for k in range(levels - 2, -1, -1):
        first_ref[k] = inverse_ref[k] * product
        product = product * second_ref[k]


def factors(upper, lower, surface_gain):
    own, levels, width = upper.shape
    return pl.pallas_call(
        functools.partial(factor_kernel, levels, own),
        out_shape=(
            jax.ShapeDtypeStruct((levels + 1, own, width), F32),
            jax.ShapeDtypeStruct((2 * levels, own, width), F32),
        ),
        in_specs=[hbm()] * 3,
        out_specs=(vmem(), vmem()),
        scratch_shapes=[
            pltpu.VMEM((own * levels, width), F32),
            pltpu.VMEM((own * levels, width), F32),
            pltpu.VMEM((own, width), F32),
            pltpu.VMEM((levels, own, width), F32),
            pltpu.SemaphoreType.DMA((3,)),
        ],
        compiler_params=params(MOST),
        cost_estimate=pl.CostEstimate(flops=1000000, bytes_accessed=400000, transcendentals=30000),
        name="factors",
    )(upper.reshape(own * levels, width), lower.reshape(own * levels, width), surface_gain)


def fetch_fields(me, groups, own, fields_ref, held_ref, sem):
    shares = fields_ref.shape[1]
    for f in range(shares):
        for q in range(groups):
            base = lax.rem(me - q + groups, groups) * own
            for i in range(own):
                pltpu.make_async_copy(
                    fields_ref.at[base + i, f], held_ref.at[f, :, q * own + i, :], sem.at[f]
                ).start()


def bottom_kernel(groups, own, rows, me_ref, place_ref, *refs):
    parts, fields_ref, send_ref, held_ref, weight_ref, value_ref, own_ref, sem, own_sem = (
        refs[:groups], *refs[groups:]
    )
    fetch = pltpu.make_async_copy(parts[0], own_ref, own_sem)
    fetch.start()
    fetch_fields(me_ref[0], groups, own, fields_ref, held_ref, sem)
    blocks = groups * own
    levels = held_ref.shape[1]
    shares = held_ref.shape[0]
    for q in range(1, groups):
        weight_ref[:, q * own:(q + 1) * own, :] = parts[q][...]
    fetch.wait()
    weight_ref[:, :own, :] = own_ref[...]
    value_ref[...] = jnp.zeros_like(value_ref)
    value_ref[pl.ds(shares, blocks, stride=rows), :] = weight_ref[levels]
    for f in range(shares):
        pltpu.make_async_copy(held_ref.at[f], held_ref.at[f], sem.at[f]).wait()
        sums = [None] * 4
        for k in range(levels):
            term = weight_ref[k] * held_ref[f, k]
            sums[k % 4] = term if sums[k % 4] is None else sums[k % 4] + term
        value_ref[pl.ds(f, blocks, stride=rows), :] = (sums[0] + sums[1]) + (sums[2] + sums[3])
    owners, slot_rows = send_ref.shape[:2]
    slots = slot_rows // rows
    for d in range(owners):
        for p in range(slots):
            start = pl.multiple_of(place_ref[d * slots + p] * rows, rows)
            send_ref[d, p * rows:(p + 1) * rows, :] = value_ref[pl.ds(start, rows), :]


def bottoms(me, place, parts, fields, owners, slots, rows):
    blocks, shares, levels, width = fields.shape
    groups = len(parts)
    own = blocks // groups
    return pl.pallas_call(
        functools.partial(bottom_kernel, groups, own, rows),
        out_shape=jax.ShapeDtypeStruct((owners, slots * rows, width), F32),
        in_specs=[smem(), smem(), hbm()] + [vmem()] * (groups - 1) + [hbm()],
        out_specs=vmem(),
        scratch_shapes=[
            pltpu.VMEM((shares, levels, blocks, width), F32),
            pltpu.VMEM((levels + 1, blocks, width), F32),
            pltpu.VMEM(((blocks + 1) * rows, width), F32),
            pltpu.VMEM((levels + 1, own, width), F32),
            pltpu.SemaphoreType.DMA((shares,)),
            pltpu.SemaphoreType.DMA(()),
        ],
        compiler_params=params(ROOMY),
        cost_estimate=pl.CostEstimate(flops=4000000, bytes_accessed=7000000, transcendentals=0),
        name="bottoms",
    )(me, place, *parts, fields)


def split_kernel(weight_ref, out_ref):
    high, low = split(weight_ref[...])
    size = weight_ref.shape[1]
    out_ref[:, :size, :] = high
    out_ref[:, size:, :] = low


def split_weights(weight, step=8):
    margins, cells, columns = weight.shape
    step = math.gcd(step, margins)
    return pl.pallas_call(
        split_kernel,
        grid=(margins // step,),
        out_shape=jax.ShapeDtypeStruct((margins, 2 * cells, columns), BF16),
        in_specs=[pl.BlockSpec((step, cells, columns), lambda i: (i, 0, 0))],
        out_specs=pl.BlockSpec((step, 2 * cells, columns), lambda i: (i, 0, 0)),
        compiler_params=params(ROOMY),
        cost_estimate=pl.CostEstimate(flops=5000000, bytes_accessed=13000000, transcendentals=0),
        name="split_weights",
    )(weight)


def margin_kernel(
    groups, rows, slots, gain_row, unroll,
    slot_ref, block_ref, count_ref, weight_hbm, got_ref, surface_ref, coef_ref, mask_ref, land_ref,
    reply_ref, flux_ref,
    weight_ref, value_ref, cell_ref, two_ref, back_ref, sem,
):
    margins = weight_ref.shape[0]
    chunks = sem.shape[0]
    size = margins // chunks
    for c in range(chunks):
        pltpu.make_async_copy(
            weight_hbm.at[pl.ds(c * size, size)], weight_ref.at[pl.ds(c * size, size)], sem.at[c]
        ).start()
    tall = groups * rows
    columns = weight_ref.shape[2]
    sources = value_ref.shape[0] // slots
    cells = surface_ref.shape[0]
    count = count_ref[0]
    for a in range(sources):
        for p in range(slots):
            for g in range(groups):
                high, low = split(got_ref[a * groups + g, p * rows:(p + 1) * rows, :])
                value_ref[a * slots + p, g * rows:(g + 1) * rows, :] = high
                value_ref[a * slots + p, tall + g * rows:tall + (g + 1) * rows, :] = low
    cell_ref[...] = jnp.zeros_like(cell_ref)
    back_ref[...] = jnp.zeros_like(back_ref)

    for c in range(chunks):
        pltpu.make_async_copy(
            weight_hbm.at[pl.ds(c * size, size)], weight_ref.at[pl.ds(c * size, size)], sem.at[c]
        ).wait()

        @pl.loop(0, size // unroll)
        def _(step):
            for u in range(unroll):
                k = c * size + step * unroll + u
                target = jnp.where(k < count, block_ref[k], cells)
                product = lax.dot_general(
                    value_ref[slot_ref[k]], weight_ref[k], (((1,), (1,)), ((), ())),
                    preferred_element_type=F32,
                )
                cell_ref[target] += (
                    product[:tall, :columns] + (product[tall:, :columns] + product[:tall, columns:])
                )

    for j in range(cells):
        cell = cell_ref[j]
        coef = coef_ref[j:j + 1, :]
        land = mask_ref[j:j + 1, :].astype(F32) * land_ref[j:j + 1, :]
        scale = coef / (1.0 + coef * (cell[gain_row:gain_row + 1, :] + land))
        flux = scale * (surface_ref[j] - cell)
        flux_ref[j] = flux
        high, low = split(flux)
        two_ref[j, :tall, :columns] = high
        two_ref[j, :tall, columns:] = high
        two_ref[j, tall:, :columns] = low
        two_ref[j, tall:, columns:] = low

    @pl.loop(0, margins // unroll)
    def _(step):
        for u in range(unroll):
            k = step * unroll + u
            target = jnp.where(k < count, slot_ref[k], sources * slots)
            product = lax.dot_general(
                two_ref[block_ref[k]], weight_ref[k], (((1,), (0,)), ((), ())),
                preferred_element_type=F32,
            )
            back_ref[target] += product[:tall] + product[tall:]

    for a in range(sources):
        for p in range(slots):
            for g in range(groups):
                reply_ref[a * groups + g, p * rows:(p + 1) * rows, :] = (
                    back_ref[a * slots + p, g * rows:(g + 1) * rows, :]
                )


def margins_stage(slot, block, count, weights, got, surface, coef, mask, land, groups, rows, slots, gain_row):
    owners, _, width = got.shape
    cells, tall, _ = surface.shape
    sources = owners // groups
    unroll = 4
    chunks = 6
    return pl.pallas_call(
        functools.partial(margin_kernel, groups, rows, slots, gain_row, unroll),
        out_shape=(
            jax.ShapeDtypeStruct(got.shape, F32),
            jax.ShapeDtypeStruct(surface.shape, F32),
        ),
        in_specs=[smem()] * 3 + [hbm()] + [vmem()] * 5,
        out_specs=(vmem(), vmem()),
        scratch_shapes=[
            pltpu.VMEM(weights.shape, BF16),
            pltpu.VMEM((sources * slots, 2 * tall, width), BF16),
            pltpu.VMEM((cells + 1, tall, width), F32),
            pltpu.VMEM((cells, 2 * tall, 2 * width), BF16),
            pltpu.VMEM((sources * slots + 1, tall, width), F32),
            pltpu.SemaphoreType.DMA((chunks,)),
        ],
        compiler_params=params(ROOMY),
        cost_estimate=pl.CostEstimate(flops=800000000, bytes_accessed=8000000, transcendentals=0),
        name="margins",
    )(slot, block, count, weights, got, surface, coef, mask, land)


def finish_kernel(groups, own, rows, me_ref, place_ref, answer_ref, *refs):
    parts, gains, fields_ref, out_ref, held_ref, factor_ref, gain_ref, flux_ref, sem, out_sem = (
        refs[:groups], refs[groups:2 * groups], *refs[2 * groups:]
    )
    me = me_ref[0]
    fetch_fields(me, groups, own, fields_ref, held_ref, sem)
    shares, levels, blocks, width = held_ref.shape
    for q in range(groups):
        factor_ref[levels:, q * own:(q + 1) * own, :] = parts[q][...]
        gain_ref[q * own:(q + 1) * own, :] = gains[q][levels]
    above = jnp.zeros((blocks, width), F32)
    for k in range(levels):
        carry = factor_ref[2 * levels + k]
        factor_ref[k] = 1.0 - carry - factor_ref[levels + k] * (1.0 - above)
        above = carry
    flux_ref[...] = jnp.zeros_like(flux_ref)
    owners, slot_rows = answer_ref.shape[:2]
    slots = slot_rows // rows
    for d in range(owners):
        for p in range(slots):
            start = pl.multiple_of(place_ref[d * slots + p] * rows, rows)
            flux_ref[pl.ds(start, rows), :] += answer_ref[d, p * rows:(p + 1) * rows, :]
    for f in range(shares):
        flux = flux_ref[pl.ds(f, blocks, stride=rows), :]
        pltpu.make_async_copy(held_ref.at[f], held_ref.at[f], sem.at[f]).wait()
        state = factor_ref[0] * held_ref[f, 0]
        held_ref[f, 0] = state
        for k in range(1, levels):
            state = factor_ref[k] * held_ref[f, k] + factor_ref[levels + k] * state
            if k < levels - 1:
                held_ref[f, k] = state
        state = state + gain_ref[...] * flux
        held_ref[f, levels - 1] = state
        for k in range(levels - 2, -1, -1):
            state = held_ref[f, k] + factor_ref[2 * levels + k] * state
            held_ref[f, k] = state
        for q in range(groups):
            base = lax.rem(me - q + groups, groups) * own
            for i in range(own):
                pltpu.make_async_copy(
                    held_ref.at[f, :, q * own + i, :], out_ref.at[base + i, f], out_sem.at[f]
                ).start()
    for f in range(shares):
        pltpu.make_async_copy(held_ref.at[f], held_ref.at[f], out_sem.at[f]).wait()


def finish(me, place, answer, parts, gains, fields, rows):
    blocks, shares, levels, width = fields.shape
    groups = len(parts)
    return pl.pallas_call(
        functools.partial(finish_kernel, groups, blocks // groups, rows),
        out_shape=jax.ShapeDtypeStruct((blocks, shares, levels, width), F32),
        in_specs=[smem(), smem(), vmem()] + [vmem()] * (2 * groups) + [hbm()],
        out_specs=hbm(),
        scratch_shapes=[
            pltpu.VMEM((shares, levels, blocks, width), F32),
            pltpu.VMEM((3 * levels, blocks, width), F32),
            pltpu.VMEM((blocks, width), F32),
            pltpu.VMEM(((blocks + 1) * rows, width), F32),
            pltpu.SemaphoreType.DMA((shares,)),
            pltpu.SemaphoreType.DMA((shares,)),
        ],
        compiler_params=params(ROOMY),
        cost_estimate=pl.CostEstimate(flops=8000000, bytes_accessed=12000000, transcendentals=0),
        name="finish",
    )(me, place, answer, *parts, *gains, fields)


def per_device(
    fields_now, upper, lower, surface_gain, route, margin_slot, margin_block, margin_count,
    margin_weight, surface_value, exchange_coef, land_mask, land_gain,
):
    groups = lax.axis_size("xg")
    me = lax.axis_index("xg").astype(jnp.int32)
    blocks, _, shares, width = fields_now.shape
    own = blocks // groups
    rows = round_up(shares + 1, ROWS)
    owners, slots = route.shape[1:]
    cells = surface_value.shape[0]

    def shift(array, by):
        return lax.ppermute(array, "xg", [(i, (i + by) % groups) for i in range(groups)])

    def shared(array):
        return [array] + [shift(array, by) for by in range(1, groups)]

    fields = fields_now.transpose(0, 2, 1, 3)
    first, second = factors(upper, lower, surface_gain)
    firsts = shared(first)
    routing = route[0].reshape(owners * slots)
    place = jnp.where(
        routing < blocks,
        lax.rem(me - routing // own + groups, groups) * own + routing % own,
        blocks,
    ).astype(jnp.int32)
    me = me[None]
    weights = split_weights(margin_weight[0])
    surface = jnp.pad(
        surface_value.reshape(cells, groups, shares, width),
        ((0, 0), (0, 0), (0, rows - shares), (0, 0)),
    ).reshape(cells, groups * rows, width)
    send = bottoms(me, place, firsts, fields, owners, slots, rows)
    got = lax.all_to_all(send, ("atm", "xg"), split_axis=0, concat_axis=0, tiled=True)
    seconds = shared(second)
    reply, flux = margins_stage(
        margin_slot[0], margin_block[0], margin_count, weights, got, surface,
        exchange_coef, land_mask, land_gain, groups, rows, slots, shares,
    )
    answer = lax.all_to_all(reply, ("atm", "xg"), split_axis=0, concat_axis=0, tiled=True)
    surface_flux = flux.reshape(cells, groups, rows, width)[:, :, :shares].reshape(
        cells, groups * shares, width
    )
    out = finish(me, place, answer, seconds, firsts, fields, rows)
    return out.transpose(0, 2, 1, 3), surface_flux


def solution(mesh):
    in_specs = (
        P("atm", None, "xg", None),
        P(("atm", "xg"), None, None),
        P(("atm", "xg"), None, None),
        P(("atm", "xg"), None),
        P("atm", None, None),
        P(("atm", "xg"), None),
        P(("atm", "xg"), None),
        P(("atm", "xg")),
        P(("atm", "xg"), None, None, None),
        P(("atm", "xg"), None, None),
        P(("atm", "xg"), None),
        P(("atm", "xg"), None),
        P(("atm", "xg"), None),
    )
    out_specs = (P("atm", None, "xg", None), P(("atm", "xg"), None, None))
    return jax.shard_map(
        per_device, mesh=mesh, in_specs=in_specs, out_specs=out_specs, check_vma=False
    )
```

```python
import functools
import math

import jax
import jax.numpy as jnp
from jax import lax
from jax.experimental import pallas as pl
from jax.experimental.pallas import tpu as pltpu
from jax.sharding import PartitionSpec as P

F32 = jnp.float32
BF16 = jnp.bfloat16
ROWS = 8
MOST = 67043328
ROOMY = 50 << 20


def vmem():
    return pl.BlockSpec(memory_space=pltpu.VMEM)


def smem():
    return pl.BlockSpec(memory_space=pltpu.SMEM)


def hbm():
    return pl.BlockSpec(memory_space=pltpu.HBM)


def params(limit):
    return pltpu.CompilerParams(vmem_limit_bytes=limit)


def round_up(value, step):
    return -(-value // step) * step


def split(value):
    high = value.astype(BF16)
    low = (value - high.astype(F32)).astype(BF16)
    return high, low


def factor_kernel(levels, own, upper_hbm, lower_hbm, gain_hbm, first_ref, second_ref,
                  upper_ref, lower_ref, gain_ref, inverse_ref, sem):
    copies = [
        pltpu.make_async_copy(source, target, sem.at[i])
        for i, (source, target) in enumerate(
            ((upper_hbm, upper_ref), (lower_hbm, lower_ref), (gain_hbm, gain_ref))
        )
    ]
    for copy in copies:
        copy.start()
    for copy in copies:
        copy.wait()
    carried = jnp.zeros(gain_ref.shape, F32)
    for k in range(levels):
        from_above = upper_ref[pl.ds(k, own, stride=levels), :] if k > 0 else jnp.zeros_like(carried)
        from_below = lower_ref[pl.ds(k, own, stride=levels), :] if k < levels - 1 else jnp.zeros_like(carried)
        inverse = 1.0 / (1.0 + from_above + from_below - from_above * carried)
        carried = from_below * inverse
        inverse_ref[k] = inverse
        second_ref[k] = from_above * inverse
        second_ref[levels + k] = carried
    product = inverse_ref[levels - 1]
    first_ref[levels] = gain_ref[...] * product
    first_ref[levels - 1] = product
    product = second_ref[levels - 1]
    for k in range(levels - 2, -1, -1):
        first_ref[k] = inverse_ref[k] * product
        product = product * second_ref[k]


def factors(upper, lower, surface_gain):
    own, levels, width = upper.shape
    return pl.pallas_call(
        functools.partial(factor_kernel, levels, own),
        out_shape=(
            jax.ShapeDtypeStruct((levels + 1, own, width), F32),
            jax.ShapeDtypeStruct((2 * levels, own, width), F32),
        ),
        in_specs=[hbm()] * 3,
        out_specs=(vmem(), vmem()),
        scratch_shapes=[
            pltpu.VMEM((own * levels, width), F32),
            pltpu.VMEM((own * levels, width), F32),
            pltpu.VMEM((own, width), F32),
            pltpu.VMEM((levels, own, width), F32),
            pltpu.SemaphoreType.DMA((3,)),
        ],
        compiler_params=params(MOST),
        cost_estimate=pl.CostEstimate(flops=1000000, bytes_accessed=400000, transcendentals=30000),
        name="factors",
    )(upper.reshape(own * levels, width), lower.reshape(own * levels, width), surface_gain)


def fetch_fields(me, groups, own, fields_ref, held_ref, sem):
    shares = fields_ref.shape[1]
    for f in range(shares):
        for q in range(groups):
            base = lax.rem(me - q + groups, groups) * own
            for i in range(own):
                pltpu.make_async_copy(
                    fields_ref.at[base + i, f], held_ref.at[f, :, q * own + i, :], sem.at[f]
                ).start()


def bottom_kernel(groups, own, rows, me_ref, place_ref, *refs):
    parts, fields_ref, send_ref, held_ref, weight_ref, value_ref, own_ref, sem, own_sem = (
        refs[:groups], *refs[groups:]
    )
    fetch = pltpu.make_async_copy(parts[0], own_ref, own_sem)
    fetch.start()
    fetch_fields(me_ref[0], groups, own, fields_ref, held_ref, sem)
    blocks = groups * own
    levels = held_ref.shape[1]
    shares = held_ref.shape[0]
    for q in range(1, groups):
        weight_ref[:, q * own:(q + 1) * own, :] = parts[q][...]
    fetch.wait()
    weight_ref[:, :own, :] = own_ref[...]
    value_ref[...] = jnp.zeros_like(value_ref)
    value_ref[pl.ds(shares, blocks, stride=rows), :] = weight_ref[levels]
    for f in range(shares):
        pltpu.make_async_copy(held_ref.at[f], held_ref.at[f], sem.at[f]).wait()
        sums = [None] * 4
        for k in range(levels):
            term = weight_ref[k] * held_ref[f, k]
            sums[k % 4] = term if sums[k % 4] is None else sums[k % 4] + term
        value_ref[pl.ds(f, blocks, stride=rows), :] = (sums[0] + sums[1]) + (sums[2] + sums[3])
    owners, slot_rows = send_ref.shape[:2]
    slots = slot_rows // rows
    for d in range(owners):
        for p in range(slots):
            start = pl.multiple_of(place_ref[d * slots + p] * rows, rows)
            send_ref[d, p * rows:(p + 1) * rows, :] = value_ref[pl.ds(start, rows), :]


def bottoms(me, place, parts, fields, owners, slots, rows):
    blocks, shares, levels, width = fields.shape
    groups = len(parts)
    own = blocks // groups
    return pl.pallas_call(
        functools.partial(bottom_kernel, groups, own, rows),
        out_shape=jax.ShapeDtypeStruct((owners, slots * rows, width), F32),
        in_specs=[smem(), smem(), hbm()] + [vmem()] * (groups - 1) + [hbm()],
        out_specs=vmem(),
        scratch_shapes=[
            pltpu.VMEM((shares, levels, blocks, width), F32),
            pltpu.VMEM((levels + 1, blocks, width), F32),
            pltpu.VMEM(((blocks + 1) * rows, width), F32),
            pltpu.VMEM((levels + 1, own, width), F32),
            pltpu.SemaphoreType.DMA((shares,)),
            pltpu.SemaphoreType.DMA(()),
        ],
        compiler_params=params(ROOMY),
        cost_estimate=pl.CostEstimate(flops=4000000, bytes_accessed=7000000, transcendentals=0),
        name="bottoms",
    )(me, place, *parts, fields)


def split_kernel(weight_ref, out_ref):
    high, low = split(weight_ref[...])
    size = weight_ref.shape[1]
    out_ref[:, :size, :] = high
    out_ref[:, size:, :] = low


def split_weights(weight, part, parts, step=8):
    margins, cells, columns = weight.shape
    count = margins // parts
    step = math.gcd(step, count)
    first = part * (count // step)
    return pl.pallas_call(
        split_kernel,
        grid=(count // step,),
        out_shape=jax.ShapeDtypeStruct((count, 2 * cells, columns), BF16),
        in_specs=[pl.BlockSpec((step, cells, columns), lambda i: (first + i, 0, 0))],
        out_specs=pl.BlockSpec((step, 2 * cells, columns), lambda i: (i, 0, 0)),
        compiler_params=params(ROOMY),
        cost_estimate=pl.CostEstimate(flops=2500000, bytes_accessed=6500000, transcendentals=0),
        name="split_weights",
    )(weight)


def margin_kernel(
    groups, rows, slots, gain_row, unroll,
    slot_ref, block_ref, count_ref, weight_a, weight_b, got_ref, surface_ref, coef_ref, mask_ref, land_ref,
    reply_ref, flux_ref,
    weight_ref, value_ref, cell_ref, two_ref, back_ref, sem,
):
    margins = weight_ref.shape[0]
    chunks = sem.shape[0]
    size = margins // chunks
    half = chunks // 2

    def fetch(c):
        source = weight_a if c < half else weight_b
        return pltpu.make_async_copy(
            source.at[pl.ds(c % half * size, size)], weight_ref.at[pl.ds(c * size, size)], sem.at[c]
        )

    for c in range(chunks):
        fetch(c).start()
    tall = groups * rows
    columns = weight_ref.shape[2]
    sources = value_ref.shape[0] // slots
    cells = surface_ref.shape[0]
    count = count_ref[0]
    for a in range(sources):
        for p in range(slots):
            for g in range(groups):
                high, low = split(got_ref[a * groups + g, p * rows:(p + 1) * rows, :])
                value_ref[a * slots + p, g * rows:(g + 1) * rows, :] = high
                value_ref[a * slots + p, tall + g * rows:tall + (g + 1) * rows, :] = low
    cell_ref[...] = jnp.zeros_like(cell_ref)
    back_ref[...] = jnp.zeros_like(back_ref)

    for c in range(chunks):
        fetch(c).wait()

        @pl.loop(0, size // unroll)
        def _(step):
            for u in range(unroll):
                k = c * size + step * unroll + u
                target = jnp.where(k < count, block_ref[k], cells)
                one = lax.dot_general(
                    value_ref[slot_ref[k]], weight_ref[k, :columns], (((1,), (1,)), ((), ())),
                    preferred_element_type=F32,
                )
                two = lax.dot_general(
                    value_ref[slot_ref[k], :tall], weight_ref[k, columns:], (((1,), (1,)), ((), ())),
                    preferred_element_type=F32,
                )
                cell_ref[target] += one[:tall] + (one[tall:] + two)

    for j in range(cells):
        cell = cell_ref[j]
        coef = coef_ref[j:j + 1, :]
        land = mask_ref[j:j + 1, :].astype(F32) * land_ref[j:j + 1, :]
        scale = coef / (1.0 + coef * (cell[gain_row:gain_row + 1, :] + land))
        flux = scale * (surface_ref[j] - cell)
        flux_ref[j] = flux
        high, low = split(flux)
        two_ref[j, :tall, :] = high
        two_ref[j, tall:, :] = low

    @pl.loop(0, margins // unroll)
    def _(step):
        for u in range(unroll):
            k = step * unroll + u
            target = jnp.where(k < count, slot_ref[k], sources * slots)
            one = jnp.dot(two_ref[block_ref[k]], weight_ref[k, :columns], preferred_element_type=F32)
            two = jnp.dot(
                two_ref[block_ref[k], :tall], weight_ref[k, columns:], preferred_element_type=F32
            )
            back_ref[target] += one[:tall] + (one[tall:] + two)

    for a in range(sources):
        for p in range(slots):
            for g in range(groups):
                reply_ref[a * groups + g, p * rows:(p + 1) * rows, :] = (
                    back_ref[a * slots + p, g * rows:(g + 1) * rows, :]
                )


def margins_stage(slot, block, count, weights_a, weights_b, got, surface, coef, mask, land,
                  groups, rows, slots, gain_row):
    half, twice, columns = weights_a.shape
    margins = 2 * half
    owners, _, width = got.shape
    cells, tall, _ = surface.shape
    sources = owners // groups
    chunks = 6
    unroll = math.gcd(16, margins // chunks)
    return pl.pallas_call(
        functools.partial(margin_kernel, groups, rows, slots, gain_row, unroll),
        out_shape=(
            jax.ShapeDtypeStruct(got.shape, F32),
            jax.ShapeDtypeStruct(surface.shape, F32),
        ),
        in_specs=[smem()] * 3 + [hbm()] * 2 + [vmem()] * 5,
        out_specs=(vmem(), vmem()),
        scratch_shapes=[
            pltpu.VMEM((margins, twice, columns), BF16),
            pltpu.VMEM((sources * slots, 2 * tall, width), BF16),
            pltpu.VMEM((cells + 1, tall, width), F32),
            pltpu.VMEM((cells, 2 * tall, width), BF16),
            pltpu.VMEM((sources * slots + 1, tall, width), F32),
            pltpu.SemaphoreType.DMA((chunks,)),
        ],
        compiler_params=params(ROOMY),
        cost_estimate=pl.CostEstimate(flops=800000000, bytes_accessed=8000000, transcendentals=0),
        name="margins",
    )(slot, block, count, weights_a, weights_b, got, surface, coef, mask, land)


def finish_kernel(groups, own, rows, me_ref, place_ref, answer_ref, *refs):
    parts, gains, fields_ref, out_ref, held_ref, factor_ref, gain_ref, flux_ref, sem, out_sem = (
        refs[:groups], refs[groups:2 * groups], *refs[2 * groups:]
    )
    me = me_ref[0]
    fetch_fields(me, groups, own, fields_ref, held_ref, sem)
    shares, levels, blocks, width = held_ref.shape
    for q in range(groups):
        factor_ref[levels:, q * own:(q + 1) * own, :] = parts[q][...]
        gain_ref[q * own:(q + 1) * own, :] = gains[q][levels]
    above = jnp.zeros((blocks, width), F32)
    for k in range(levels):
        carry = factor_ref[2 * levels + k]
        factor_ref[k] = 1.0 - carry - factor_ref[levels + k] * (1.0 - above)
        above = carry
    flux_ref[...] = jnp.zeros_like(flux_ref)
    owners, slot_rows = answer_ref.shape[:2]
    slots = slot_rows // rows
    for d in range(owners):
        for p in range(slots):
            start = pl.multiple_of(place_ref[d * slots + p] * rows, rows)
            flux_ref[pl.ds(start, rows), :] += answer_ref[d, p * rows:(p + 1) * rows, :]
    for f in range(shares):
        flux = flux_ref[pl.ds(f, blocks, stride=rows), :]
        pltpu.make_async_copy(held_ref.at[f], held_ref.at[f], sem.at[f]).wait()
        state = factor_ref[0] * held_ref[f, 0]
        held_ref[f, 0] = state
        for k in range(1, levels):
            state = factor_ref[k] * held_ref[f, k] + factor_ref[levels + k] * state
            if k < levels - 1:
                held_ref[f, k] = state
        state = state + gain_ref[...] * flux
        held_ref[f, levels - 1] = state
        for k in range(levels - 2, -1, -1):
            state = held_ref[f, k] + factor_ref[2 * levels + k] * state
            held_ref[f, k] = state
        for q in range(groups):
            base = lax.rem(me - q + groups, groups) * own
            for i in range(own):
                pltpu.make_async_copy(
                    held_ref.at[f, :, q * own + i, :], out_ref.at[base + i, f], out_sem.at[f]
                ).start()
    for f in range(shares):
        pltpu.make_async_copy(held_ref.at[f], held_ref.at[f], out_sem.at[f]).wait()


def finish(me, place, answer, parts, gains, fields, rows):
    blocks, shares, levels, width = fields.shape
    groups = len(parts)
    return pl.pallas_call(
        functools.partial(finish_kernel, groups, blocks // groups, rows),
        out_shape=jax.ShapeDtypeStruct((blocks, shares, levels, width), F32),
        in_specs=[smem(), smem(), vmem()] + [vmem()] * (2 * groups) + [hbm()],
        out_specs=hbm(),
        scratch_shapes=[
            pltpu.VMEM((shares, levels, blocks, width), F32),
            pltpu.VMEM((3 * levels, blocks, width), F32),
            pltpu.VMEM((blocks, width), F32),
            pltpu.VMEM(((blocks + 1) * rows, width), F32),
            pltpu.SemaphoreType.DMA((shares,)),
            pltpu.SemaphoreType.DMA((shares,)),
        ],
        compiler_params=params(ROOMY),
        cost_estimate=pl.CostEstimate(flops=8000000, bytes_accessed=12000000, transcendentals=0),
        name="finish",
    )(me, place, answer, *parts, *gains, fields)


def per_device(
    fields_now, upper, lower, surface_gain, route, margin_slot, margin_block, margin_count,
    margin_weight, surface_value, exchange_coef, land_mask, land_gain,
):
    groups = lax.axis_size("xg")
    me = lax.axis_index("xg").astype(jnp.int32)
    blocks, _, shares, width = fields_now.shape
    own = blocks // groups
    rows = round_up(shares + 1, ROWS)
    owners, slots = route.shape[1:]
    cells = surface_value.shape[0]

    def shift(array, by):
        return lax.ppermute(array, "xg", [(i, (i + by) % groups) for i in range(groups)])

    def shared(array):
        return [array] + [shift(array, by) for by in range(1, groups)]

    fields = fields_now.transpose(0, 2, 1, 3)
    first, second = factors(upper, lower, surface_gain)
    firsts = shared(first)
    routing = route[0].reshape(owners * slots)
    place = jnp.where(
        routing < blocks,
        lax.rem(me - routing // own + groups, groups) * own + routing % own,
        blocks,
    ).astype(jnp.int32)
    me = me[None]
    weights_a = split_weights(margin_weight[0], 0, 2)
    weights_b = split_weights(margin_weight[0], 1, 2)
    surface = jnp.pad(
        surface_value.reshape(cells, groups, shares, width),
        ((0, 0), (0, 0), (0, rows - shares), (0, 0)),
    ).reshape(cells, groups * rows, width)
    send = bottoms(me, place, firsts, fields, owners, slots, rows)
    got = lax.all_to_all(send, ("atm", "xg"), split_axis=0, concat_axis=0, tiled=True)
    seconds = shared(second)
    reply, flux = margins_stage(
        margin_slot[0], margin_block[0], margin_count, weights_a, weights_b, got, surface,
        exchange_coef, land_mask, land_gain, groups, rows, slots, shares,
    )
    answer = lax.all_to_all(reply, ("atm", "xg"), split_axis=0, concat_axis=0, tiled=True)
    surface_flux = flux.reshape(cells, groups, rows, width)[:, :, :shares].reshape(
        cells, groups * shares, width
    )
    out = finish(me, place, answer, seconds, firsts, fields, rows)
    return out.transpose(0, 2, 1, 3), surface_flux


def solution(mesh):
    in_specs = (
        P("atm", None, "xg", None),
        P(("atm", "xg"), None, None),
        P(("atm", "xg"), None, None),
        P(("atm", "xg"), None),
        P("atm", None, None),
        P(("atm", "xg"), None),
        P(("atm", "xg"), None),
        P(("atm", "xg")),
        P(("atm", "xg"), None, None, None),
        P(("atm", "xg"), None, None),
        P(("atm", "xg"), None),
        P(("atm", "xg"), None),
        P(("atm", "xg"), None),
    )
    out_specs = (P("atm", None, "xg", None), P(("atm", "xg"), None, None))
    return jax.shard_map(
        per_device, mesh=mesh, in_specs=in_specs, out_specs=out_specs, check_vma=False
    )
```

```python
import functools
import math

import jax
import jax.numpy as jnp
from jax import lax
from jax.experimental import pallas as pl
from jax.experimental.pallas import tpu as pltpu
from jax.sharding import PartitionSpec as P

F32 = jnp.float32
BF16 = jnp.bfloat16
ROWS = 8
MOST = 67043328
ROOMY = 50 << 20


def vmem():
    return pl.BlockSpec(memory_space=pltpu.VMEM)


def smem():
    return pl.BlockSpec(memory_space=pltpu.SMEM)


def hbm():
    return pl.BlockSpec(memory_space=pltpu.HBM)


def params(limit):
    return pltpu.CompilerParams(vmem_limit_bytes=limit)


def round_up(value, step):
    return -(-value // step) * step


def split(value):
    high = value.astype(BF16).astype(F32)
    return jnp.concatenate([high, value - high], 0).astype(BF16)


def factor_kernel(levels, own, upper_hbm, lower_hbm, gain_hbm, first_ref, second_ref,
                  upper_ref, lower_ref, gain_ref, sem):
    copies = [
        pltpu.make_async_copy(source, target, sem.at[i])
        for i, (source, target) in enumerate(
            ((upper_hbm, upper_ref), (lower_hbm, lower_ref), (gain_hbm, gain_ref))
        )
    ]
    for copy in copies:
        copy.start()
    for copy in copies:
        copy.wait()
    carried = jnp.zeros(gain_ref.shape, F32)
    inverse = carried
    for k in range(levels):
        from_above = upper_ref[pl.ds(k, own, stride=levels), :] if k > 0 else jnp.zeros_like(carried)
        from_below = lower_ref[pl.ds(k, own, stride=levels), :] if k < levels - 1 else jnp.zeros_like(carried)
        if k > 0:
            first_ref[k] = from_above * inverse
        inverse = 1.0 / (1.0 + from_above + from_below - from_above * carried)
        carried = from_below * inverse
        second_ref[k] = carried
    first_ref[0] = inverse
    first_ref[levels] = gain_ref[...] * inverse


def factors(upper, lower, surface_gain):
    own, levels, width = upper.shape
    return pl.pallas_call(
        functools.partial(factor_kernel, levels, own),
        out_shape=(
            jax.ShapeDtypeStruct((levels + 1, own, width), F32),
            jax.ShapeDtypeStruct((levels, own, width), F32),
        ),
        in_specs=[hbm()] * 3,
        out_specs=(vmem(), vmem()),
        scratch_shapes=[
            pltpu.VMEM((own * levels, width), F32),
            pltpu.VMEM((own * levels, width), F32),
            pltpu.VMEM((own, width), F32),
            pltpu.SemaphoreType.DMA((3,)),
        ],
        compiler_params=params(MOST),
        cost_estimate=pl.CostEstimate(flops=1000000, bytes_accessed=400000, transcendentals=30000),
        name="factors",
    )(upper.reshape(own * levels, width), lower.reshape(own * levels, width), surface_gain)


def fetch_fields(me, groups, own, fields_ref, held_ref, sem):
    shares = fields_ref.shape[1]
    for f in range(shares):
        for q in range(groups):
            base = lax.rem(me - q + groups, groups) * own
            for i in range(own):
                pltpu.make_async_copy(
                    fields_ref.at[base + i, f], held_ref.at[f, :, q * own + i, :], sem.at[f]
                ).start()


def bottom_kernel(groups, own, rows, slots, me_ref, place_ref, *refs):
    parts, fields_ref, send_ref, held_ref, weight_ref, value_ref, own_ref, sem, own_sem = (
        refs[:groups], *refs[groups:]
    )
    fetch = pltpu.make_async_copy(parts[0], own_ref, own_sem)
    fetch.start()
    fetch_fields(me_ref[0], groups, own, fields_ref, held_ref, sem)
    blocks = groups * own
    pitch = round_up(rows, ROWS)
    levels = held_ref.shape[1]
    shares = held_ref.shape[0]
    for q in range(1, groups):
        weight_ref[:, q * own:(q + 1) * own, :] = parts[q][...]
    fetch.wait()
    weight_ref[:, :own, :] = own_ref[...]
    weight = weight_ref[0]
    for k in range(levels - 1, -1, -1):
        ratio = weight_ref[k]
        weight_ref[k] = weight
        weight = weight * ratio
    value_ref[...] = jnp.zeros_like(value_ref)
    value_ref[pl.ds(shares, blocks, stride=pitch), :] = weight_ref[levels]
    for f in range(shares):
        pltpu.make_async_copy(held_ref.at[f], held_ref.at[f], sem.at[f]).wait()
        sums = [None] * 4
        for k in range(levels):
            term = weight_ref[k] * held_ref[f, k]
            sums[k % 4] = term if sums[k % 4] is None else sums[k % 4] + term
        value_ref[pl.ds(f, blocks, stride=pitch), :] = (sums[0] + sums[1]) + (sums[2] + sums[3])
    for d in range(send_ref.shape[0] // (rows * slots)):
        for p in range(slots):
            start = pl.multiple_of(place_ref[d * slots + p] * pitch, pitch)
            send_ref[pl.ds(d * rows * slots + p, rows, stride=slots), :] = value_ref[pl.ds(start, rows), :]


def bottoms(me, place, parts, fields, owners, slots, rows):
    blocks, shares, levels, width = fields.shape
    groups = len(parts)
    own = blocks // groups
    return pl.pallas_call(
        functools.partial(bottom_kernel, groups, own, rows, slots),
        out_shape=jax.ShapeDtypeStruct((owners * rows * slots, width), F32),
        in_specs=[smem(), smem(), hbm()] + [vmem()] * (groups - 1) + [hbm()],
        out_specs=vmem(),
        scratch_shapes=[
            pltpu.VMEM((shares, levels, blocks, width), F32),
            pltpu.VMEM((levels + 1, blocks, width), F32),
            pltpu.VMEM(((blocks + 1) * round_up(rows, ROWS), width), F32),
            pltpu.VMEM((levels + 1, own, width), F32),
            pltpu.SemaphoreType.DMA((shares,)),
            pltpu.SemaphoreType.DMA(()),
        ],
        compiler_params=params(ROOMY),
        cost_estimate=pl.CostEstimate(flops=4000000, bytes_accessed=7000000, transcendentals=0),
        name="bottoms",
    )(me, place, *parts, fields)


def split_kernel(weight_ref, out_ref):
    value = weight_ref[...]
    size = weight_ref.shape[1]
    high = value.astype(BF16)
    out_ref[:, :size, :] = high
    out_ref[:, size:, :] = (value - high.astype(F32)).astype(BF16)


def split_weights(weight, part, parts, step=8):
    margins, cells, columns = weight.shape
    count = margins // parts
    step = math.gcd(step, count)
    first = part * (count // step)
    return pl.pallas_call(
        split_kernel,
        grid=(count // step,),
        out_shape=jax.ShapeDtypeStruct((count, 2 * cells, columns), BF16),
        in_specs=[pl.BlockSpec((step, cells, columns), lambda i: (first + i, 0, 0))],
        out_specs=pl.BlockSpec((step, 2 * cells, columns), lambda i: (i, 0, 0)),
        compiler_params=params(ROOMY),
        cost_estimate=pl.CostEstimate(flops=2500000, bytes_accessed=6500000, transcendentals=0),
        name="split_weights",
    )(weight)


def margin_kernel(
    groups, rows, slots, gain_row, unroll,
    slot_ref, block_ref, count_ref, weight_a, weight_b, got_ref, surface_ref, coef_ref, mask_ref, land_ref,
    reply_ref, flux_ref,
    weight_ref, value_ref, cell_ref, two_ref, back_ref, stack_ref, sem,
):
    margins = weight_ref.shape[0]
    chunks = sem.shape[0]
    size = margins // chunks
    half = chunks // 2

    def fetch(c):
        source = weight_a if c < half else weight_b
        return pltpu.make_async_copy(
            source.at[pl.ds(c % half * size, size)], weight_ref.at[pl.ds(c * size, size)], sem.at[c]
        )

    for c in range(chunks):
        fetch(c).start()
    tall = groups * rows
    top = round_up(tall, 2 * ROWS)
    columns = weight_ref.shape[2]
    sources = value_ref.shape[0] // slots
    cells = surface_ref.shape[0]
    count = count_ref[0]
    for a in range(sources):
        for p in range(slots):
            for g in range(groups):
                stack_ref[a * slots + p, g * rows:(g + 1) * rows, :] = (
                    got_ref[pl.ds((a * groups + g) * rows * slots + p, rows, stride=slots), :]
                )
    for s in range(sources * slots):
        value_ref[s] = split(stack_ref[s])
    cell_ref[...] = jnp.zeros_like(cell_ref)
    back_ref[...] = jnp.zeros_like(back_ref)

    for c in range(chunks):
        fetch(c).wait()

        @pl.loop(0, size // unroll)
        def _(step):
            for u in range(unroll):
                k = c * size + step * unroll + u
                target = jnp.where(k < count, block_ref[k], cells)
                one = lax.dot_general(
                    value_ref[slot_ref[k]], weight_ref[k, :columns], (((1,), (1,)), ((), ())),
                    preferred_element_type=F32,
                )
                two = lax.dot_general(
                    value_ref[slot_ref[k], :top], weight_ref[k, columns:], (((1,), (1,)), ((), ())),
                    preferred_element_type=F32,
                )
                cell_ref[target] += one[:tall] + (one[tall:] + two[:tall])

    for j in range(cells):
        cell = cell_ref[j]
        coef = coef_ref[j:j + 1, :]
        land = mask_ref[j:j + 1, :].astype(F32) * land_ref[j:j + 1, :]
        scale = coef / (1.0 + coef * (cell[gain_row:gain_row + 1, :] + land))
        flux = scale * (surface_ref[j] - cell)
        flux_ref[j] = flux
        two_ref[j] = split(flux)

    @pl.loop(0, margins // unroll)
    def _(step):
        for u in range(unroll):
            k = step * unroll + u
            target = jnp.where(k < count, slot_ref[k], sources * slots)
            one = jnp.dot(two_ref[block_ref[k]], weight_ref[k, :columns], preferred_element_type=F32)
            two = jnp.dot(
                two_ref[block_ref[k], :top], weight_ref[k, columns:], preferred_element_type=F32
            )
            back_ref[target] += one[:tall] + (one[tall:] + two[:tall])

    for a in range(sources):
        for p in range(slots):
            for g in range(groups):
                reply_ref[pl.ds((a * groups + g) * rows * slots + p, rows, stride=slots), :] = (
                    back_ref[a * slots + p, g * rows:(g + 1) * rows, :]
                )


def margins_stage(slot, block, count, weights_a, weights_b, got, surface, coef, mask, land,
                  groups, rows, slots, gain_row):
    half, twice, columns = weights_a.shape
    margins = 2 * half
    width = got.shape[1]
    owners = got.shape[0] // (rows * slots)
    cells, tall, _ = surface.shape
    sources = owners // groups
    chunks = 6
    unroll = math.gcd(16, margins // chunks)
    return pl.pallas_call(
        functools.partial(margin_kernel, groups, rows, slots, gain_row, unroll),
        out_shape=(
            jax.ShapeDtypeStruct(got.shape, F32),
            jax.ShapeDtypeStruct(surface.shape, F32),
        ),
        in_specs=[smem()] * 3 + [hbm()] * 2 + [vmem()] * 5,
        out_specs=(vmem(), vmem()),
        scratch_shapes=[
            pltpu.VMEM((margins, twice, columns), BF16),
            pltpu.VMEM((sources * slots, 2 * tall, width), BF16),
            pltpu.VMEM((cells + 1, tall, width), F32),
            pltpu.VMEM((cells, 2 * tall, width), BF16),
            pltpu.VMEM((sources * slots + 1, tall, width), F32),
            pltpu.VMEM((sources * slots, tall, width), F32),
            pltpu.SemaphoreType.DMA((chunks,)),
        ],
        compiler_params=params(ROOMY),
        cost_estimate=pl.CostEstimate(flops=800000000, bytes_accessed=8000000, transcendentals=0),
        name="margins",
    )(slot, block, count, weights_a, weights_b, got, surface, coef, mask, land)


def unfold_kernel(groups, own, *refs):
    firsts, seconds, after_ref, factor_ref, gain_ref = (
        refs[:groups], refs[groups:2 * groups], *refs[2 * groups:]
    )
    levels = factor_ref.shape[0] // 3
    for q in range(groups):
        factor_ref[:levels, q * own:(q + 1) * own, :] = firsts[q][:levels]
        factor_ref[2 * levels:, q * own:(q + 1) * own, :] = seconds[q][...]
        gain_ref[q * own:(q + 1) * own, :] = firsts[q][levels]
    above = factor_ref[2 * levels]
    inverse = 1.0 - above
    factor_ref[levels] = inverse
    for k in range(1, levels):
        carry = factor_ref[2 * levels + k]
        inverse = (1.0 - carry) * inverse / (inverse + factor_ref[k] * (1.0 - above))
        factor_ref[levels + k] = inverse
        above = carry


def unfold(firsts, seconds, after):
    levels, own, width = seconds[0].shape
    groups = len(seconds)
    blocks = groups * own
    return pl.pallas_call(
        functools.partial(unfold_kernel, groups, own),
        out_shape=(
            jax.ShapeDtypeStruct((3 * levels, blocks, width), F32),
            jax.ShapeDtypeStruct((blocks, width), F32),
        ),
        in_specs=[vmem()] * (2 * groups) + [hbm()],
        out_specs=(vmem(), vmem()),
        compiler_params=params(ROOMY),
        cost_estimate=pl.CostEstimate(flops=1000000, bytes_accessed=3000000, transcendentals=100000),
        name="unfold",
    )(*firsts, *seconds, after)


def finish_kernel(groups, own, rows, slots, me_ref, place_ref, answer_ref, factor_ref, gain_ref,
                  fields_ref, out_ref, held_ref, flux_ref, sem, out_sem):
    me = me_ref[0]
    fetch_fields(me, groups, own, fields_ref, held_ref, sem)
    shares, levels, blocks, _ = held_ref.shape
    flux_ref[...] = jnp.zeros_like(flux_ref)
    pitch = round_up(rows, ROWS)
    for d in range(answer_ref.shape[0] // (rows * slots)):
        for p in range(slots):
            start = pl.multiple_of(place_ref[d * slots + p] * pitch, pitch)
            flux_ref[pl.ds(start, rows), :] += (
                answer_ref[pl.ds(d * rows * slots + p, rows, stride=slots), :]
            )
    for f in range(shares):
        flux = flux_ref[pl.ds(f, blocks, stride=pitch), :]
        pltpu.make_async_copy(held_ref.at[f], held_ref.at[f], sem.at[f]).wait()
        state = held_ref[f, 0]
        for k in range(1, levels):
            state = held_ref[f, k] + factor_ref[k] * state
            if k < levels - 1:
                held_ref[f, k] = state
        state = factor_ref[2 * levels - 1] * state + gain_ref[...] * flux
        held_ref[f, levels - 1] = state
        for k in range(levels - 2, -1, -1):
            state = factor_ref[levels + k] * held_ref[f, k] + factor_ref[2 * levels + k] * state
            held_ref[f, k] = state
        for q in range(groups):
            base = lax.rem(me - q + groups, groups) * own
            for i in range(own):
                pltpu.make_async_copy(
                    held_ref.at[f, :, q * own + i, :], out_ref.at[base + i, f], out_sem.at[f]
                ).start()
    for f in range(shares):
        pltpu.make_async_copy(held_ref.at[f], held_ref.at[f], out_sem.at[f]).wait()


def finish(me, place, answer, factor, gain, fields, groups, rows, slots):
    blocks, shares, levels, width = fields.shape
    return pl.pallas_call(
        functools.partial(finish_kernel, groups, blocks // groups, rows, slots),
        out_shape=jax.ShapeDtypeStruct((blocks, shares, levels, width), F32),
        in_specs=[smem(), smem(), vmem(), vmem(), vmem(), hbm()],
        out_specs=hbm(),
        scratch_shapes=[
            pltpu.VMEM((shares, levels, blocks, width), F32),
            pltpu.VMEM(((blocks + 1) * round_up(rows, ROWS), width), F32),
            pltpu.SemaphoreType.DMA((shares,)),
            pltpu.SemaphoreType.DMA((shares,)),
        ],
        compiler_params=params(ROOMY),
        cost_estimate=pl.CostEstimate(flops=8000000, bytes_accessed=12000000, transcendentals=0),
        name="finish",
    )(me, place, answer, factor, gain, fields)


def per_device(
    fields_now, upper, lower, surface_gain, route, margin_slot, margin_block, margin_count,
    margin_weight, surface_value, exchange_coef, land_mask, land_gain,
):
    groups = lax.axis_size("xg")
    me = lax.axis_index("xg").astype(jnp.int32)
    blocks, _, shares, width = fields_now.shape
    own = blocks // groups
    rows = shares + 1
    owners, slots = route.shape[1:]
    cells = surface_value.shape[0]

    def shift(array, by):
        return lax.ppermute(array, "xg", [(i, (i + by) % groups) for i in range(groups)])

    def shared(array):
        return [array] + [shift(array, by) for by in range(1, groups)]

    def exchange(array):
        array = array.reshape(owners, rows, slots, width)
        array = lax.all_to_all(array, ("atm", "xg"), split_axis=0, concat_axis=0, tiled=True)
        return array.reshape(owners * rows * slots, width)

    fields = fields_now.transpose(0, 2, 1, 3)
    first, second = factors(upper, lower, surface_gain)
    firsts = shared(first)
    routing = route[0].reshape(owners * slots)
    place = jnp.where(
        routing < blocks,
        lax.rem(me - routing // own + groups, groups) * own + routing % own,
        blocks,
    ).astype(jnp.int32)
    me = me[None]
    weights_a = split_weights(margin_weight[0], 0, 2)
    weights_b = split_weights(margin_weight[0], 1, 2)
    surface = jnp.pad(
        surface_value.reshape(cells, groups, shares, width),
        ((0, 0), (0, 0), (0, rows - shares), (0, 0)),
    ).reshape(cells, groups * rows, width)
    send = bottoms(me, place, firsts, fields, owners, slots, rows)
    got = exchange(send)
    seconds = shared(second)
    reply, flux = margins_stage(
        margin_slot[0], margin_block[0], margin_count, weights_a, weights_b, got, surface,
        exchange_coef, land_mask, land_gain, groups, rows, slots, shares,
    )
    answer = exchange(reply)
    surface_flux = flux.reshape(cells, groups, rows, width)[:, :, :shares].reshape(
        cells, groups * shares, width
    )
    factor, gain = unfold(firsts, seconds, reply)
    out = finish(me, place, answer, factor, gain, fields, groups, rows, slots)
    return out.transpose(0, 2, 1, 3), surface_flux


def solution(mesh):
    in_specs = (
        P("atm", None, "xg", None),
        P(("atm", "xg"), None, None),
        P(("atm", "xg"), None, None),
        P(("atm", "xg"), None),
        P("atm", None, None),
        P(("atm", "xg"), None),
        P(("atm", "xg"), None),
        P(("atm", "xg")),
        P(("atm", "xg"), None, None, None),
        P(("atm", "xg"), None, None),
        P(("atm", "xg"), None),
        P(("atm", "xg"), None),
        P(("atm", "xg"), None),
    )
    out_specs = (P("atm", None, "xg", None), P(("atm", "xg"), None, None))
    return jax.shard_map(
        per_device, mesh=mesh, in_specs=in_specs, out_specs=out_specs, check_vma=False
    )
```

```python
import functools
import math

import jax
import jax.numpy as jnp
from jax import lax
from jax.experimental import pallas as pl
from jax.experimental.pallas import tpu as pltpu
from jax.sharding import PartitionSpec as P

F32 = jnp.float32
BF16 = jnp.bfloat16
ROWS = 8
MOST = 67043328
ROOMY = 50 << 20


def vmem():
    return pl.BlockSpec(memory_space=pltpu.VMEM)


def smem():
    return pl.BlockSpec(memory_space=pltpu.SMEM)


def hbm():
    return pl.BlockSpec(memory_space=pltpu.HBM)


def params(limit):
    return pltpu.CompilerParams(vmem_limit_bytes=limit)


def round_up(value, step):
    return -(-value // step) * step


def split(value):
    high = value.astype(BF16).astype(F32)
    return jnp.concatenate([high, value - high], 0).astype(BF16)


def factor_kernel(levels, own, upper_hbm, lower_hbm, gain_hbm, first_ref, second_ref,
                  upper_ref, lower_ref, gain_ref, sem):
    copies = [
        pltpu.make_async_copy(source, target, sem.at[i])
        for i, (source, target) in enumerate(
            ((upper_hbm, upper_ref), (lower_hbm, lower_ref), (gain_hbm, gain_ref))
        )
    ]
    for copy in copies:
        copy.start()
    for copy in copies:
        copy.wait()
    carried = jnp.zeros(gain_ref.shape, F32)
    inverse = carried
    for k in range(levels):
        from_above = upper_ref[pl.ds(k, own, stride=levels), :] if k > 0 else jnp.zeros_like(carried)
        from_below = lower_ref[pl.ds(k, own, stride=levels), :] if k < levels - 1 else jnp.zeros_like(carried)
        if k > 0:
            first_ref[k] = from_above * inverse
        inverse = 1.0 / (1.0 + from_above + from_below - from_above * carried)
        carried = from_below * inverse
        second_ref[k] = carried
    first_ref[0] = inverse
    first_ref[levels] = gain_ref[...] * inverse


def factors(upper, lower, surface_gain):
    own, levels, width = upper.shape
    return pl.pallas_call(
        functools.partial(factor_kernel, levels, own),
        out_shape=(
            jax.ShapeDtypeStruct((levels + 1, own, width), F32),
            jax.ShapeDtypeStruct((levels, own, width), F32),
        ),
        in_specs=[hbm()] * 3,
        out_specs=(vmem(), vmem()),
        scratch_shapes=[
            pltpu.VMEM((own * levels, width), F32),
            pltpu.VMEM((own * levels, width), F32),
            pltpu.VMEM((own, width), F32),
            pltpu.SemaphoreType.DMA((3,)),
        ],
        compiler_params=params(MOST),
        cost_estimate=pl.CostEstimate(flops=1000000, bytes_accessed=400000, transcendentals=30000),
        name="factors",
    )(upper.reshape(own * levels, width), lower.reshape(own * levels, width), surface_gain)


def fetch_fields(me, groups, own, fields_ref, held_ref, sem):
    shares = fields_ref.shape[1]
    for f in range(shares):
        for q in range(groups):
            base = lax.rem(me - q + groups, groups) * own
            for i in range(own):
                pltpu.make_async_copy(
                    fields_ref.at[base + i, f], held_ref.at[f, :, q * own + i, :], sem.at[f]
                ).start()


def bottom_kernel(groups, own, rows, slots, me_ref, place_ref, *refs):
    parts, fields_ref, send_ref, held_ref, weight_ref, value_ref, own_ref, sem, own_sem = (
        refs[:groups], *refs[groups:]
    )
    fetch = pltpu.make_async_copy(parts[0], own_ref, own_sem)
    fetch.start()
    fetch_fields(me_ref[0], groups, own, fields_ref, held_ref, sem)
    blocks = groups * own
    pitch = round_up(rows, ROWS)
    levels = held_ref.shape[1]
    shares = held_ref.shape[0]
    for q in range(1, groups):
        weight_ref[:, q * own:(q + 1) * own, :] = parts[q][...]
    fetch.wait()
    weight_ref[:, :own, :] = own_ref[...]
    weight = weight_ref[0]
    for k in range(levels - 1, -1, -1):
        ratio = weight_ref[k]
        weight_ref[k] = weight
        weight = weight * ratio
    value_ref[...] = jnp.zeros_like(value_ref)
    value_ref[pl.ds(shares, blocks, stride=pitch), :] = weight_ref[levels]
    for f in range(shares):
        pltpu.make_async_copy(held_ref.at[f], held_ref.at[f], sem.at[f]).wait()
        sums = [None] * 4
        for k in range(levels):
            term = weight_ref[k] * held_ref[f, k]
            sums[k % 4] = term if sums[k % 4] is None else sums[k % 4] + term
        value_ref[pl.ds(f, blocks, stride=pitch), :] = (sums[0] + sums[1]) + (sums[2] + sums[3])
    for d in range(send_ref.shape[0] // (rows * slots)):
        for p in range(slots):
            start = pl.multiple_of(place_ref[d * slots + p] * pitch, pitch)
            send_ref[pl.ds(d * rows * slots + p, rows, stride=slots), :] = value_ref[pl.ds(start, rows), :]


def bottoms(me, place, parts, fields, owners, slots, rows):
    blocks, shares, levels, width = fields.shape
    groups = len(parts)
    own = blocks // groups
    return pl.pallas_call(
        functools.partial(bottom_kernel, groups, own, rows, slots),
        out_shape=jax.ShapeDtypeStruct((owners * rows * slots, width), F32),
        in_specs=[smem(), smem(), hbm()] + [vmem()] * (groups - 1) + [hbm()],
        out_specs=vmem(),
        scratch_shapes=[
            pltpu.VMEM((shares, levels, blocks, width), F32),
            pltpu.VMEM((levels + 1, blocks, width), F32),
            pltpu.VMEM(((blocks + 1) * round_up(rows, ROWS), width), F32),
            pltpu.VMEM((levels + 1, own, width), F32),
            pltpu.SemaphoreType.DMA((shares,)),
            pltpu.SemaphoreType.DMA(()),
        ],
        compiler_params=params(ROOMY),
        cost_estimate=pl.CostEstimate(flops=4000000, bytes_accessed=7000000, transcendentals=0),
        name="bottoms",
    )(me, place, *parts, fields)


def split_kernel(weight_ref, out_ref):
    value = weight_ref[...]
    size = weight_ref.shape[1]
    high = value.astype(BF16)
    out_ref[:, :size, :] = high
    out_ref[:, size:, :] = (value - high.astype(F32)).astype(BF16)


def split_weights(weight, part, parts, step=8):
    margins, cells, columns = weight.shape
    count = margins // parts
    step = math.gcd(step, count)
    first = part * (count // step)
    return pl.pallas_call(
        split_kernel,
        grid=(count // step,),
        out_shape=jax.ShapeDtypeStruct((count, 2 * cells, columns), BF16),
        in_specs=[pl.BlockSpec((step, cells, columns), lambda i: (first + i, 0, 0))],
        out_specs=pl.BlockSpec((step, 2 * cells, columns), lambda i: (i, 0, 0)),
        compiler_params=params(ROOMY),
        cost_estimate=pl.CostEstimate(flops=2500000, bytes_accessed=6500000, transcendentals=0),
        name="split_weights",
    )(weight)


def margin_kernel(
    groups, rows, slots, gain_row, unroll,
    slot_ref, block_ref, count_ref, weight_a, weight_b, got_ref, surface_ref, coef_ref, mask_ref, land_ref,
    reply_ref, flux_ref,
    weight_ref, value_ref, cell_ref, two_ref, back_ref, stack_ref, sem,
):
    margins = weight_ref.shape[0]
    chunks = sem.shape[0]
    size = margins // chunks
    half = chunks // 2

    def fetch(c):
        source = weight_a if c < half else weight_b
        return pltpu.make_async_copy(
            source.at[pl.ds(c % half * size, size)], weight_ref.at[pl.ds(c * size, size)], sem.at[c]
        )

    for c in range(chunks):
        fetch(c).start()
    tall = groups * rows
    top = round_up(tall, 2 * ROWS)
    columns = weight_ref.shape[2]
    sources = value_ref.shape[0] // slots
    cells = surface_ref.shape[0]
    count = count_ref[0]
    for a in range(sources):
        for p in range(slots):
            for g in range(groups):
                stack_ref[a * slots + p, g * rows:(g + 1) * rows, :] = (
                    got_ref[pl.ds((a * groups + g) * rows * slots + p, rows, stride=slots), :]
                )
    for s in range(sources * slots):
        value_ref[s] = split(stack_ref[s])
    cell_ref[...] = jnp.zeros_like(cell_ref)
    back_ref[...] = jnp.zeros_like(back_ref)

    for c in range(chunks):
        fetch(c).wait()

        @pl.loop(0, size // unroll)
        def _(step):
            for u in range(unroll):
                k = c * size + step * unroll + u
                target = jnp.where(k < count, block_ref[k], cells)
                one = lax.dot_general(
                    value_ref[slot_ref[k]], weight_ref[k, :columns], (((1,), (1,)), ((), ())),
                    preferred_element_type=F32,
                )
                two = lax.dot_general(
                    value_ref[slot_ref[k], :top], weight_ref[k, columns:], (((1,), (1,)), ((), ())),
                    preferred_element_type=F32,
                )
                cell_ref[target] += one[:tall] + (one[tall:] + two[:tall])

    for j in range(cells):
        cell = cell_ref[j]
        coef = coef_ref[j:j + 1, :]
        land = mask_ref[j:j + 1, :].astype(F32) * land_ref[j:j + 1, :]
        scale = coef / (1.0 + coef * (cell[gain_row:gain_row + 1, :] + land))
        flux = scale * (surface_ref[j] - cell)
        flux_ref[j] = flux
        two_ref[j] = split(flux)

    @pl.loop(0, margins // unroll)
    def _(step):
        for u in range(unroll):
            k = step * unroll + u
            target = jnp.where(k < count, slot_ref[k], sources * slots)
            one = jnp.dot(two_ref[block_ref[k]], weight_ref[k, :columns], preferred_element_type=F32)
            two = jnp.dot(
                two_ref[block_ref[k], :top], weight_ref[k, columns:], preferred_element_type=F32
            )
            back_ref[target] += one[:tall] + (one[tall:] + two[:tall])

    for a in range(sources):
        for p in range(slots):
            for g in range(groups):
                reply_ref[pl.ds((a * groups + g) * rows * slots + p, rows, stride=slots), :] = (
                    back_ref[a * slots + p, g * rows:(g + 1) * rows, :]
                )


def margins_stage(slot, block, count, weights_a, weights_b, got, surface, coef, mask, land,
                  groups, rows, slots, gain_row):
    half, twice, columns = weights_a.shape
    margins = 2 * half
    width = got.shape[1]
    owners = got.shape[0] // (rows * slots)
    cells, tall, _ = surface.shape
    sources = owners // groups
    chunks = 6
    unroll = math.gcd(16, margins // chunks)
    return pl.pallas_call(
        functools.partial(margin_kernel, groups, rows, slots, gain_row, unroll),
        out_shape=(
            jax.ShapeDtypeStruct(got.shape, F32),
            jax.ShapeDtypeStruct(surface.shape, F32),
        ),
        in_specs=[smem()] * 3 + [hbm()] * 2 + [vmem()] * 5,
        out_specs=(vmem(), vmem()),
        scratch_shapes=[
            pltpu.VMEM((margins, twice, columns), BF16),
            pltpu.VMEM((sources * slots, 2 * tall, width), BF16),
            pltpu.VMEM((cells + 1, tall, width), F32),
            pltpu.VMEM((cells, 2 * tall, width), BF16),
            pltpu.VMEM((sources * slots + 1, tall, width), F32),
            pltpu.VMEM((sources * slots, tall, width), F32),
            pltpu.SemaphoreType.DMA((chunks,)),
        ],
        compiler_params=params(ROOMY),
        cost_estimate=pl.CostEstimate(flops=800000000, bytes_accessed=8000000, transcendentals=0),
        name="margins",
    )(slot, block, count, weights_a, weights_b, got, surface, coef, mask, land)


def unfold_kernel(groups, own, *refs):
    firsts, seconds, after_ref, factor_ref, gain_ref = (
        refs[:groups], refs[groups:2 * groups], *refs[2 * groups:]
    )
    levels = factor_ref.shape[0] // 3
    for q in range(groups):
        factor_ref[:levels, q * own:(q + 1) * own, :] = firsts[q][:levels]
        factor_ref[2 * levels:, q * own:(q + 1) * own, :] = seconds[q][...]
        gain_ref[q * own:(q + 1) * own, :] = firsts[q][levels]
    above = factor_ref[2 * levels]
    inverse = 1.0 - above
    factor_ref[levels] = inverse
    for k in range(1, levels):
        carry = factor_ref[2 * levels + k]
        inverse = (1.0 - carry) * inverse / (inverse + factor_ref[k] * (1.0 - above))
        factor_ref[levels + k] = inverse
        above = carry


def unfold(firsts, seconds, after):
    levels, own, width = seconds[0].shape
    groups = len(seconds)
    blocks = groups * own
    return pl.pallas_call(
        functools.partial(unfold_kernel, groups, own),
        out_shape=(
            jax.ShapeDtypeStruct((3 * levels, blocks, width), F32),
            jax.ShapeDtypeStruct((blocks, width), F32),
        ),
        in_specs=[vmem()] * (2 * groups) + [hbm()],
        out_specs=(vmem(), vmem()),
        compiler_params=params(ROOMY),
        cost_estimate=pl.CostEstimate(flops=1000000, bytes_accessed=3000000, transcendentals=100000),
        name="unfold",
    )(*firsts, *seconds, after)


def finish_kernel(groups, own, rows, slots, me_ref, place_ref, answer_ref, factor_ref, gain_ref,
                  fields_ref, out_ref, held_ref, flux_ref, sem, out_sem):
    me = me_ref[0]
    fetch_fields(me, groups, own, fields_ref, held_ref, sem)
    shares, levels, blocks, _ = held_ref.shape
    flux_ref[...] = jnp.zeros_like(flux_ref)
    pitch = round_up(rows, ROWS)
    for d in range(answer_ref.shape[0] // (rows * slots)):
        for p in range(slots):
            start = pl.multiple_of(place_ref[d * slots + p] * pitch, pitch)
            flux_ref[pl.ds(start, rows), :] += (
                answer_ref[pl.ds(d * rows * slots + p, rows, stride=slots), :]
            )
    for f in range(shares):
        flux = flux_ref[pl.ds(f, blocks, stride=pitch), :]
        pltpu.make_async_copy(held_ref.at[f], held_ref.at[f], sem.at[f]).wait()
        state = held_ref[f, 0]
        for k in range(1, levels):
            state = held_ref[f, k] + factor_ref[k] * state
            if k < levels - 1:
                held_ref[f, k] = state
        state = factor_ref[2 * levels - 1] * state + gain_ref[...] * flux
        held_ref[f, levels - 1] = state
        for k in range(levels - 2, -1, -1):
            state = factor_ref[levels + k] * held_ref[f, k] + factor_ref[2 * levels + k] * state
            held_ref[f, k] = state
        for q in range(groups):
            base = lax.rem(me - q + groups, groups) * own
            for i in range(own):
                pltpu.make_async_copy(
                    held_ref.at[f, :, q * own + i, :], out_ref.at[base + i, f], out_sem.at[f]
                ).start()
    for f in range(shares):
        pltpu.make_async_copy(held_ref.at[f], held_ref.at[f], out_sem.at[f]).wait()


def finish(me, place, answer, factor, gain, fields, groups, rows, slots):
    blocks, shares, levels, width = fields.shape
    return pl.pallas_call(
        functools.partial(finish_kernel, groups, blocks // groups, rows, slots),
        out_shape=jax.ShapeDtypeStruct((blocks, shares, levels, width), F32),
        in_specs=[smem(), smem(), vmem(), vmem(), vmem(), hbm()],
        out_specs=hbm(),
        scratch_shapes=[
            pltpu.VMEM((shares, levels, blocks, width), F32),
            pltpu.VMEM(((blocks + 1) * round_up(rows, ROWS), width), F32),
            pltpu.SemaphoreType.DMA((shares,)),
            pltpu.SemaphoreType.DMA((shares,)),
        ],
        compiler_params=params(ROOMY),
        cost_estimate=pl.CostEstimate(flops=8000000, bytes_accessed=12000000, transcendentals=0),
        name="finish",
    )(me, place, answer, factor, gain, fields)


def per_device(
    fields_now, upper, lower, surface_gain, route, margin_slot, margin_block, margin_count,
    margin_weight, surface_value, exchange_coef, land_mask, land_gain,
):
    groups = lax.axis_size("xg")
    me = lax.axis_index("xg").astype(jnp.int32)
    blocks, _, shares, width = fields_now.shape
    own = blocks // groups
    rows = shares + 1
    owners, slots = route.shape[1:]
    cells = surface_value.shape[0]

    def shift(array, by):
        return lax.ppermute(array, "xg", [(i, (i + by) % groups) for i in range(groups)])

    def shared(array):
        return [array] + [shift(array, by) for by in range(1, groups)]

    def exchange(array):
        array = array.reshape(owners, rows, slots, width)
        array = lax.all_to_all(array, ("atm", "xg"), split_axis=0, concat_axis=0, tiled=True)
        return array.reshape(owners * rows * slots, width)

    fields = fields_now.transpose(0, 2, 1, 3)
    first, second = factors(upper, lower, surface_gain)
    firsts = shared(first)
    routing = route[0].reshape(owners * slots)
    place = jnp.where(
        routing < blocks,
        lax.rem(me - routing // own + groups, groups) * own + routing % own,
        blocks,
    ).astype(jnp.int32)
    me = me[None]
    weights_a = split_weights(margin_weight[0], 0, 2)
    weights_b = split_weights(margin_weight[0], 1, 2)
    surface = jnp.pad(
        surface_value.reshape(cells, groups, shares, width),
        ((0, 0), (0, 0), (0, rows - shares), (0, 0)),
    ).reshape(cells, groups * rows, width)
    send = bottoms(me, place, firsts, fields, owners, slots, rows)
    got = exchange(send)
    up, down = shift(second, 1), shift(second, groups - 1)
    seconds = [second, up] + [None] * (groups - 3) + [down]
    for by in range(groups - 2, 1, -1):
        seconds[by] = shift(seconds[by + 1], groups - 1)
    reply, flux = margins_stage(
        margin_slot[0], margin_block[0], margin_count, weights_a, weights_b, got, surface,
        exchange_coef, land_mask, land_gain, groups, rows, slots, shares,
    )
    answer = exchange(reply)
    surface_flux = flux.reshape(cells, groups, rows, width)[:, :, :shares].reshape(
        cells, groups * shares, width
    )
    factor, gain = unfold(firsts, seconds, reply)
    out = finish(me, place, answer, factor, gain, fields, groups, rows, slots)
    return out.transpose(0, 2, 1, 3), surface_flux


def solution(mesh):
    in_specs = (
        P("atm", None, "xg", None),
        P(("atm", "xg"), None, None),
        P(("atm", "xg"), None, None),
        P(("atm", "xg"), None),
        P("atm", None, None),
        P(("atm", "xg"), None),
        P(("atm", "xg"), None),
        P(("atm", "xg")),
        P(("atm", "xg"), None, None, None),
        P(("atm", "xg"), None, None),
        P(("atm", "xg"), None),
        P(("atm", "xg"), None),
        P(("atm", "xg"), None),
    )
    out_specs = (P("atm", None, "xg", None), P(("atm", "xg"), None, None))
    return jax.shard_map(
        per_device, mesh=mesh, in_specs=in_specs, out_specs=out_specs, check_vma=False
    )
```

```python
import functools
import math

import jax
import jax.numpy as jnp
from jax import lax
from jax.experimental import pallas as pl
from jax.experimental.pallas import tpu as pltpu
from jax.sharding import PartitionSpec as P

F32 = jnp.float32
BF16 = jnp.bfloat16
ROWS = 8
MOST = 67043328
ROOMY = 50 << 20


def vmem():
    return pl.BlockSpec(memory_space=pltpu.VMEM)


def smem():
    return pl.BlockSpec(memory_space=pltpu.SMEM)


def hbm():
    return pl.BlockSpec(memory_space=pltpu.HBM)


def params(limit):
    return pltpu.CompilerParams(vmem_limit_bytes=limit)


def round_up(value, step):
    return -(-value // step) * step


def split(value):
    high = value.astype(BF16).astype(F32)
    return jnp.concatenate([high, value - high], 0).astype(BF16)


def factor_kernel(levels, own, upper_hbm, lower_hbm, gain_hbm, first_ref, second_ref,
                  upper_ref, lower_ref, gain_ref, sem):
    copies = [
        pltpu.make_async_copy(source, target, sem.at[i])
        for i, (source, target) in enumerate(
            ((upper_hbm, upper_ref), (lower_hbm, lower_ref), (gain_hbm, gain_ref))
        )
    ]
    for copy in copies:
        copy.start()
    for copy in copies:
        copy.wait()
    carried = jnp.zeros(gain_ref.shape, F32)
    inverse = carried
    for k in range(levels):
        from_above = upper_ref[pl.ds(k, own, stride=levels), :] if k > 0 else jnp.zeros_like(carried)
        from_below = lower_ref[pl.ds(k, own, stride=levels), :] if k < levels - 1 else jnp.zeros_like(carried)
        if k > 0:
            first_ref[k] = from_above * inverse
        inverse = 1.0 / (1.0 + from_above + from_below - from_above * carried)
        carried = from_below * inverse
        second_ref[k] = carried
    first_ref[0] = inverse
    first_ref[levels] = gain_ref[...] * inverse


def factors(upper, lower, surface_gain):
    own, levels, width = upper.shape
    return pl.pallas_call(
        functools.partial(factor_kernel, levels, own),
        out_shape=(
            jax.ShapeDtypeStruct((levels + 1, own, width), F32),
            jax.ShapeDtypeStruct((levels, own, width), F32),
        ),
        in_specs=[hbm()] * 3,
        out_specs=(vmem(), vmem()),
        scratch_shapes=[
            pltpu.VMEM((own * levels, width), F32),
            pltpu.VMEM((own * levels, width), F32),
            pltpu.VMEM((own, width), F32),
            pltpu.SemaphoreType.DMA((3,)),
        ],
        compiler_params=params(MOST),
        cost_estimate=pl.CostEstimate(flops=1000000, bytes_accessed=400000, transcendentals=30000),
        name="factors",
    )(upper.reshape(own * levels, width), lower.reshape(own * levels, width), surface_gain)


def fetch_fields(me, groups, own, fields_ref, held_ref, sem):
    shares = fields_ref.shape[1]
    for f in range(shares):
        for q in range(groups):
            base = lax.rem(me - q + groups, groups) * own
            for i in range(own):
                pltpu.make_async_copy(
                    fields_ref.at[base + i, f], held_ref.at[f, :, q * own + i, :], sem.at[f]
                ).start()


def bottom_kernel(groups, own, rows, slots, me_ref, place_ref, *refs):
    parts, fields_ref, send_ref, held_ref, weight_ref, value_ref, own_ref, sem, own_sem = (
        refs[:groups], *refs[groups:]
    )
    fetch = pltpu.make_async_copy(parts[0], own_ref, own_sem)
    fetch.start()
    fetch_fields(me_ref[0], groups, own, fields_ref, held_ref, sem)
    blocks = groups * own
    pitch = round_up(rows, ROWS)
    levels = held_ref.shape[1]
    shares = held_ref.shape[0]
    for q in range(1, groups):
        weight_ref[:, q * own:(q + 1) * own, :] = parts[q][...]
    fetch.wait()
    weight_ref[:, :own, :] = own_ref[...]
    weight = weight_ref[0]
    for k in range(levels - 1, -1, -1):
        ratio = weight_ref[k]
        weight_ref[k] = weight
        weight = weight * ratio
    value_ref[...] = jnp.zeros_like(value_ref)
    value_ref[pl.ds(shares, blocks, stride=pitch), :] = weight_ref[levels]
    for f in range(shares):
        pltpu.make_async_copy(held_ref.at[f], held_ref.at[f], sem.at[f]).wait()
        sums = [None] * 4
        for k in range(levels):
            term = weight_ref[k] * held_ref[f, k]
            sums[k % 4] = term if sums[k % 4] is None else sums[k % 4] + term
        value_ref[pl.ds(f, blocks, stride=pitch), :] = (sums[0] + sums[1]) + (sums[2] + sums[3])
    for d in range(send_ref.shape[0] // (rows * slots)):
        for p in range(slots):
            start = pl.multiple_of(place_ref[d * slots + p] * pitch, pitch)
            send_ref[pl.ds(d * rows * slots + p, rows, stride=slots), :] = value_ref[pl.ds(start, rows), :]


def bottoms(me, place, parts, fields, owners, slots, rows):
    blocks, shares, levels, width = fields.shape
    groups = len(parts)
    own = blocks // groups
    return pl.pallas_call(
        functools.partial(bottom_kernel, groups, own, rows, slots),
        out_shape=jax.ShapeDtypeStruct((owners * rows * slots, width), F32),
        in_specs=[smem(), smem(), hbm()] + [vmem()] * (groups - 1) + [hbm()],
        out_specs=vmem(),
        scratch_shapes=[
            pltpu.VMEM((shares, levels, blocks, width), F32),
            pltpu.VMEM((levels + 1, blocks, width), F32),
            pltpu.VMEM(((blocks + 1) * round_up(rows, ROWS), width), F32),
            pltpu.VMEM((levels + 1, own, width), F32),
            pltpu.SemaphoreType.DMA((shares,)),
            pltpu.SemaphoreType.DMA(()),
        ],
        compiler_params=params(ROOMY),
        cost_estimate=pl.CostEstimate(flops=4000000, bytes_accessed=7000000, transcendentals=0),
        name="bottoms",
    )(me, place, *parts, fields)


def split_kernel(weight_ref, out_ref):
    value = weight_ref[...]
    size = weight_ref.shape[1]
    high = value.astype(BF16)
    out_ref[:, :size, :] = high
    out_ref[:, size:, :] = (value - high.astype(F32)).astype(BF16)


def split_weights(weight, start, stop, step=8):
    _, cells, columns = weight.shape
    count = stop - start
    step = math.gcd(step, math.gcd(start, count))
    first = start // step
    return pl.pallas_call(
        split_kernel,
        grid=(count // step,),
        out_shape=jax.ShapeDtypeStruct((count, 2 * cells, columns), BF16),
        in_specs=[pl.BlockSpec((step, cells, columns), lambda i: (first + i, 0, 0))],
        out_specs=pl.BlockSpec((step, 2 * cells, columns), lambda i: (i, 0, 0)),
        compiler_params=params(ROOMY),
        cost_estimate=pl.CostEstimate(flops=2500000, bytes_accessed=6500000, transcendentals=0),
        name="split_weights",
    )(weight)


def margin_kernel(
    groups, rows, slots, gain_row, unroll,
    slot_ref, block_ref, count_ref, weight_a, weight_b, got_ref, surface_ref, coef_ref, mask_ref, land_ref,
    reply_ref, flux_ref,
    weight_ref, value_ref, cell_ref, two_ref, back_ref, stack_ref, sem,
):
    margins = weight_ref.shape[0]
    chunks = sem.shape[0]
    size = margins // chunks
    half = weight_a.shape[0] // size

    def fetch(c):
        source = weight_a if c < half else weight_b
        return pltpu.make_async_copy(
            source.at[pl.ds((c if c < half else c - half) * size, size)], weight_ref.at[pl.ds(c * size, size)], sem.at[c]
        )

    for c in range(chunks):
        fetch(c).start()
    tall = groups * rows
    top = round_up(tall, 2 * ROWS)
    columns = weight_ref.shape[2]
    sources = value_ref.shape[0] // slots
    cells = surface_ref.shape[0]
    count = count_ref[0]
    for a in range(sources):
        for p in range(slots):
            for g in range(groups):
                stack_ref[a * slots + p, g * rows:(g + 1) * rows, :] = (
                    got_ref[pl.ds((a * groups + g) * rows * slots + p, rows, stride=slots), :]
                )
    for s in range(sources * slots):
        value_ref[s] = split(stack_ref[s])
    cell_ref[...] = jnp.zeros_like(cell_ref)
    back_ref[...] = jnp.zeros_like(back_ref)

    for c in range(chunks):
        fetch(c).wait()

        @pl.loop(0, size // unroll)
        def _(step):
            for u in range(unroll):
                k = c * size + step * unroll + u
                target = jnp.where(k < count, block_ref[k], cells)
                one = lax.dot_general(
                    value_ref[slot_ref[k]], weight_ref[k, :columns], (((1,), (1,)), ((), ())),
                    preferred_element_type=F32,
                )
                two = lax.dot_general(
                    value_ref[slot_ref[k], :top], weight_ref[k, columns:], (((1,), (1,)), ((), ())),
                    preferred_element_type=F32,
                )
                cell_ref[target] += one[:tall] + (one[tall:] + two[:tall])

    for j in range(cells):
        cell = cell_ref[j]
        coef = coef_ref[j:j + 1, :]
        land = mask_ref[j:j + 1, :].astype(F32) * land_ref[j:j + 1, :]
        scale = coef / (1.0 + coef * (cell[gain_row:gain_row + 1, :] + land))
        flux = scale * (surface_ref[j] - cell)
        flux_ref[j] = flux
        two_ref[j] = split(flux)

    @pl.loop(0, margins // unroll)
    def _(step):
        for u in range(unroll):
            k = step * unroll + u
            target = jnp.where(k < count, slot_ref[k], sources * slots)
            one = jnp.dot(two_ref[block_ref[k]], weight_ref[k, :columns], preferred_element_type=F32)
            two = jnp.dot(
                two_ref[block_ref[k], :top], weight_ref[k, columns:], preferred_element_type=F32
            )
            back_ref[target] += one[:tall] + (one[tall:] + two[:tall])

    for a in range(sources):
        for p in range(slots):
            for g in range(groups):
                reply_ref[pl.ds((a * groups + g) * rows * slots + p, rows, stride=slots), :] = (
                    back_ref[a * slots + p, g * rows:(g + 1) * rows, :]
                )


def margins_stage(slot, block, count, weights_a, weights_b, got, surface, coef, mask, land,
                  groups, rows, slots, gain_row):
    part, twice, columns = weights_a.shape
    margins = part + weights_b.shape[0]
    width = got.shape[1]
    owners = got.shape[0] // (rows * slots)
    cells, tall, _ = surface.shape
    sources = owners // groups
    chunks = 6
    unroll = math.gcd(16, margins // chunks)
    return pl.pallas_call(
        functools.partial(margin_kernel, groups, rows, slots, gain_row, unroll),
        out_shape=(
            jax.ShapeDtypeStruct(got.shape, F32),
            jax.ShapeDtypeStruct(surface.shape, F32),
        ),
        in_specs=[smem()] * 3 + [hbm()] * 2 + [vmem()] * 5,
        out_specs=(vmem(), vmem()),
        scratch_shapes=[
            pltpu.VMEM((margins, twice, columns), BF16),
            pltpu.VMEM((sources * slots, 2 * tall, width), BF16),
            pltpu.VMEM((cells + 1, tall, width), F32),
            pltpu.VMEM((cells, 2 * tall, width), BF16),
            pltpu.VMEM((sources * slots + 1, tall, width), F32),
            pltpu.VMEM((sources * slots, tall, width), F32),
            pltpu.SemaphoreType.DMA((chunks,)),
        ],
        compiler_params=params(ROOMY),
        cost_estimate=pl.CostEstimate(flops=800000000, bytes_accessed=8000000, transcendentals=0),
        name="margins",
    )(slot, block, count, weights_a, weights_b, got, surface, coef, mask, land)


def unfold_kernel(groups, own, *refs):
    firsts, seconds, after_ref, factor_ref, gain_ref = (
        refs[:groups], refs[groups:2 * groups], *refs[2 * groups:]
    )
    levels = factor_ref.shape[0] // 3
    for q in range(groups):
        factor_ref[:levels, q * own:(q + 1) * own, :] = firsts[q][:levels]
        factor_ref[2 * levels:, q * own:(q + 1) * own, :] = seconds[q][...]
        gain_ref[q * own:(q + 1) * own, :] = firsts[q][levels]
    above = factor_ref[2 * levels]
    inverse = 1.0 - above
    factor_ref[levels] = inverse
    for k in range(1, levels):
        carry = factor_ref[2 * levels + k]
        inverse = (1.0 - carry) * inverse / (inverse + factor_ref[k] * (1.0 - above))
        factor_ref[levels + k] = inverse
        above = carry


def unfold(firsts, seconds, after):
    levels, own, width = seconds[0].shape
    groups = len(seconds)
    blocks = groups * own
    return pl.pallas_call(
        functools.partial(unfold_kernel, groups, own),
        out_shape=(
            jax.ShapeDtypeStruct((3 * levels, blocks, width), F32),
            jax.ShapeDtypeStruct((blocks, width), F32),
        ),
        in_specs=[vmem()] * (2 * groups) + [hbm()],
        out_specs=(vmem(), vmem()),
        compiler_params=params(ROOMY),
        cost_estimate=pl.CostEstimate(flops=1000000, bytes_accessed=3000000, transcendentals=100000),
        name="unfold",
    )(*firsts, *seconds, after)


def finish_kernel(groups, own, rows, slots, me_ref, place_ref, answer_ref, factor_ref, gain_ref,
                  fields_ref, out_ref, held_ref, flux_ref, sem, out_sem):
    me = me_ref[0]
    fetch_fields(me, groups, own, fields_ref, held_ref, sem)
    shares, levels, blocks, _ = held_ref.shape
    flux_ref[...] = jnp.zeros_like(flux_ref)
    pitch = round_up(rows, ROWS)
    for d in range(answer_ref.shape[0] // (rows * slots)):
        for p in range(slots):
            start = pl.multiple_of(place_ref[d * slots + p] * pitch, pitch)
            flux_ref[pl.ds(start, rows), :] += (
                answer_ref[pl.ds(d * rows * slots + p, rows, stride=slots), :]
            )
    for f in range(shares):
        flux = flux_ref[pl.ds(f, blocks, stride=pitch), :]
        pltpu.make_async_copy(held_ref.at[f], held_ref.at[f], sem.at[f]).wait()
        state = held_ref[f, 0]
        for k in range(1, levels):
            state = held_ref[f, k] + factor_ref[k] * state
            if k < levels - 1:
                held_ref[f, k] = state
        state = factor_ref[2 * levels - 1] * state + gain_ref[...] * flux
        held_ref[f, levels - 1] = state
        for k in range(levels - 2, -1, -1):
            state = factor_ref[levels + k] * held_ref[f, k] + factor_ref[2 * levels + k] * state
            held_ref[f, k] = state
        for q in range(groups):
            base = lax.rem(me - q + groups, groups) * own
            for i in range(own):
                pltpu.make_async_copy(
                    held_ref.at[f, :, q * own + i, :], out_ref.at[base + i, f], out_sem.at[f]
                ).start()
    for f in range(shares):
        pltpu.make_async_copy(held_ref.at[f], held_ref.at[f], out_sem.at[f]).wait()


def finish(me, place, answer, factor, gain, fields, groups, rows, slots):
    blocks, shares, levels, width = fields.shape
    return pl.pallas_call(
        functools.partial(finish_kernel, groups, blocks // groups, rows, slots),
        out_shape=jax.ShapeDtypeStruct((blocks, shares, levels, width), F32),
        in_specs=[smem(), smem(), vmem(), vmem(), vmem(), hbm()],
        out_specs=hbm(),
        scratch_shapes=[
            pltpu.VMEM((shares, levels, blocks, width), F32),
            pltpu.VMEM(((blocks + 1) * round_up(rows, ROWS), width), F32),
            pltpu.SemaphoreType.DMA((shares,)),
            pltpu.SemaphoreType.DMA((shares,)),
        ],
        compiler_params=params(ROOMY),
        cost_estimate=pl.CostEstimate(flops=8000000, bytes_accessed=12000000, transcendentals=0),
        name="finish",
    )(me, place, answer, factor, gain, fields)


def per_device(
    fields_now, upper, lower, surface_gain, route, margin_slot, margin_block, margin_count,
    margin_weight, surface_value, exchange_coef, land_mask, land_gain,
):
    groups = lax.axis_size("xg")
    me = lax.axis_index("xg").astype(jnp.int32)
    blocks, _, shares, width = fields_now.shape
    own = blocks // groups
    rows = shares + 1
    owners, slots = route.shape[1:]
    cells = surface_value.shape[0]

    def shift(array, by):
        return lax.ppermute(array, "xg", [(i, (i + by) % groups) for i in range(groups)])

    def shared(array):
        return [array] + [shift(array, by) for by in range(1, groups)]

    def exchange(array):
        array = array.reshape(owners, rows, slots, width)
        array = lax.all_to_all(array, ("atm", "xg"), split_axis=0, concat_axis=0, tiled=True)
        return array.reshape(owners * rows * slots, width)

    fields = fields_now.transpose(0, 2, 1, 3)
    first, second = factors(upper, lower, surface_gain)
    firsts = shared(first)
    relayed = second
    seconds = [second] + [None] * (groups - 1)
    for by in range(groups - 1, 0, -1):
        relayed = shift(relayed, groups - 1)
        seconds[by] = relayed
    routing = route[0].reshape(owners * slots)
    place = jnp.where(
        routing < blocks,
        lax.rem(me - routing // own + groups, groups) * own + routing % own,
        blocks,
    ).astype(jnp.int32)
    me = me[None]
    weights_a = split_weights(margin_weight[0], 0, margin_weight.shape[1] // 3)
    weights_b = split_weights(margin_weight[0], margin_weight.shape[1] // 3, margin_weight.shape[1])
    surface = jnp.pad(
        surface_value.reshape(cells, groups, shares, width),
        ((0, 0), (0, 0), (0, rows - shares), (0, 0)),
    ).reshape(cells, groups * rows, width)
    send = bottoms(me, place, firsts, fields, owners, slots, rows)
    got = exchange(send)
    reply, flux = margins_stage(
        margin_slot[0], margin_block[0], margin_count, weights_a, weights_b, got, surface,
        exchange_coef, land_mask, land_gain, groups, rows, slots, shares,
    )
    answer = exchange(reply)
    surface_flux = flux.reshape(cells, groups, rows, width)[:, :, :shares].reshape(
        cells, groups * shares, width
    )
    factor, gain = unfold(firsts, seconds, reply)
    out = finish(me, place, answer, factor, gain, fields, groups, rows, slots)
    return out.transpose(0, 2, 1, 3), surface_flux


def solution(mesh):
    in_specs = (
        P("atm", None, "xg", None),
        P(("atm", "xg"), None, None),
        P(("atm", "xg"), None, None),
        P(("atm", "xg"), None),
        P("atm", None, None),
        P(("atm", "xg"), None),
        P(("atm", "xg"), None),
        P(("atm", "xg")),
        P(("atm", "xg"), None, None, None),
        P(("atm", "xg"), None, None),
        P(("atm", "xg"), None),
        P(("atm", "xg"), None),
        P(("atm", "xg"), None),
    )
    out_specs = (P("atm", None, "xg", None), P(("atm", "xg"), None, None))
    return jax.shard_map(
        per_device, mesh=mesh, in_specs=in_specs, out_specs=out_specs, check_vma=False
    )
```

```python
import functools
import math

import jax
import jax.numpy as jnp
from jax import lax
from jax.experimental import pallas as pl
from jax.experimental.pallas import tpu as pltpu
from jax.sharding import PartitionSpec as P

F32 = jnp.float32
BF16 = jnp.bfloat16
ROWS = 8
PIECES = 5
MOST = 67043328
ROOMY = 50 << 20


def vmem():
    return pl.BlockSpec(memory_space=pltpu.VMEM)


def smem():
    return pl.BlockSpec(memory_space=pltpu.SMEM)


def hbm():
    return pl.BlockSpec(memory_space=pltpu.HBM)


def params(limit):
    return pltpu.CompilerParams(vmem_limit_bytes=limit)


def round_up(value, step):
    return -(-value // step) * step


def split(value):
    high = value.astype(BF16).astype(F32)
    return jnp.concatenate([high, value - high], 0).astype(BF16)


def factor_kernel(levels, own, upper_hbm, lower_hbm, gain_hbm, first_ref, second_ref,
                  upper_ref, lower_ref, gain_ref, sem):
    copies = [
        pltpu.make_async_copy(source, target, sem.at[i])
        for i, (source, target) in enumerate(
            ((upper_hbm, upper_ref), (lower_hbm, lower_ref), (gain_hbm, gain_ref))
        )
    ]
    for copy in copies:
        copy.start()
    for copy in copies:
        copy.wait()
    carried = jnp.zeros(gain_ref.shape, F32)
    inverse = carried
    for k in range(levels):
        from_above = upper_ref[pl.ds(k, own, stride=levels), :] if k > 0 else jnp.zeros_like(carried)
        from_below = lower_ref[pl.ds(k, own, stride=levels), :] if k < levels - 1 else jnp.zeros_like(carried)
        if k > 0:
            first_ref[k] = from_above * inverse
        inverse = 1.0 / (1.0 + from_above + from_below - from_above * carried)
        carried = from_below * inverse
        second_ref[k] = carried
    first_ref[0] = inverse
    first_ref[levels] = gain_ref[...] * inverse


def factors(upper, lower, surface_gain):
    own, levels, width = upper.shape
    return pl.pallas_call(
        functools.partial(factor_kernel, levels, own),
        out_shape=(
            jax.ShapeDtypeStruct((levels + 1, own, width), F32),
            jax.ShapeDtypeStruct((levels, own, width), F32),
        ),
        in_specs=[hbm()] * 3,
        out_specs=(vmem(), vmem()),
        scratch_shapes=[
            pltpu.VMEM((own * levels, width), F32),
            pltpu.VMEM((own * levels, width), F32),
            pltpu.VMEM((own, width), F32),
            pltpu.SemaphoreType.DMA((3,)),
        ],
        compiler_params=params(MOST),
        cost_estimate=pl.CostEstimate(flops=1000000, bytes_accessed=400000, transcendentals=30000),
        name="factors",
    )(upper.reshape(own * levels, width), lower.reshape(own * levels, width), surface_gain)


def bundles(shares):
    pieces = min(PIECES, shares)
    edges = [i * shares // pieces for i in range(pieces + 1)]
    return list(zip(edges[:-1], edges[1:]))


def field_copies(me, groups, own, fields_ref, held_ref, sem, piece, out):
    low, high = bundles(held_ref.shape[0])[piece]
    copies = []
    for q in range(groups):
        base = lax.rem(me - q + groups, groups) * own
        for i in range(own):
            far = fields_ref.at[base + i, pl.ds(low, high - low)]
            near = held_ref.at[pl.ds(low, high - low), :, q * own + i, :]
            pair = (near, far) if out else (far, near)
            copies.append(pltpu.make_async_copy(*pair, sem.at[piece]))
    return copies


def fetch_fields(me, groups, own, fields_ref, held_ref, sem):
    for piece in range(len(bundles(held_ref.shape[0]))):
        for copy in field_copies(me, groups, own, fields_ref, held_ref, sem, piece, False):
            copy.start()


def wait_piece(held_ref, sem, piece):
    low, high = bundles(held_ref.shape[0])[piece]
    part = held_ref.at[pl.ds(low, high - low)]
    pltpu.make_async_copy(part, part, sem.at[piece]).wait()


def bottom_kernel(groups, own, rows, slots, me_ref, place_ref, *refs):
    parts, fields_ref, send_ref, held_ref, weight_ref, value_ref, own_ref, sem, own_sem = (
        refs[:groups], *refs[groups:]
    )
    fetch = pltpu.make_async_copy(parts[0], own_ref, own_sem)
    fetch.start()
    fetch_fields(me_ref[0], groups, own, fields_ref, held_ref, sem)
    blocks = groups * own
    pitch = round_up(rows, ROWS)
    levels = held_ref.shape[1]
    shares = held_ref.shape[0]
    for q in range(1, groups):
        weight_ref[:, q * own:(q + 1) * own, :] = parts[q][...]
    fetch.wait()
    weight_ref[:, :own, :] = own_ref[...]
    weight = weight_ref[0]
    for k in range(levels - 1, -1, -1):
        ratio = weight_ref[k]
        weight_ref[k] = weight
        weight = weight * ratio
    value_ref[...] = jnp.zeros_like(value_ref)
    value_ref[pl.ds(shares, blocks, stride=pitch), :] = weight_ref[levels]
    for piece, (low, high) in enumerate(bundles(shares)):
        wait_piece(held_ref, sem, piece)
        sums = {}
        for k in range(levels):
            weight = weight_ref[k]
            for f in range(low, high):
                term = weight * held_ref[f, k]
                slot = (f, k % 2)
                sums[slot] = sums[slot] + term if slot in sums else term
        for f in range(low, high):
            value_ref[pl.ds(f, blocks, stride=pitch), :] = sums[f, 0] + sums[f, 1]
    for d in range(send_ref.shape[0] // (rows * slots)):
        for p in range(slots):
            start = pl.multiple_of(place_ref[d * slots + p] * pitch, pitch)
            send_ref[pl.ds(d * rows * slots + p, rows, stride=slots), :] = value_ref[pl.ds(start, rows), :]


def bottoms(me, place, parts, fields, owners, slots, rows):
    blocks, shares, levels, width = fields.shape
    groups = len(parts)
    own = blocks // groups
    return pl.pallas_call(
        functools.partial(bottom_kernel, groups, own, rows, slots),
        out_shape=jax.ShapeDtypeStruct((owners * rows * slots, width), F32),
        in_specs=[smem(), smem(), hbm()] + [vmem()] * (groups - 1) + [hbm()],
        out_specs=vmem(),
        scratch_shapes=[
            pltpu.VMEM((shares, levels, blocks, width), F32),
            pltpu.VMEM((levels + 1, blocks, width), F32),
            pltpu.VMEM(((blocks + 1) * round_up(rows, ROWS), width), F32),
            pltpu.VMEM((levels + 1, own, width), F32),
            pltpu.SemaphoreType.DMA((len(bundles(shares)),)),
            pltpu.SemaphoreType.DMA(()),
        ],
        compiler_params=params(ROOMY),
        cost_estimate=pl.CostEstimate(flops=4000000, bytes_accessed=7000000, transcendentals=0),
        name="bottoms",
    )(me, place, *parts, fields)


def split_kernel(weight_ref, out_ref):
    value = weight_ref[...]
    size = weight_ref.shape[1]
    high = value.astype(BF16)
    out_ref[:, :size, :] = high
    out_ref[:, size:, :] = (value - high.astype(F32)).astype(BF16)


def split_weights(weight, start, stop, step=8):
    _, cells, columns = weight.shape
    count = stop - start
    step = math.gcd(step, math.gcd(start, count))
    first = start // step
    return pl.pallas_call(
        split_kernel,
        grid=(count // step,),
        out_shape=jax.ShapeDtypeStruct((count, 2 * cells, columns), BF16),
        in_specs=[pl.BlockSpec((step, cells, columns), lambda i: (first + i, 0, 0))],
        out_specs=pl.BlockSpec((step, 2 * cells, columns), lambda i: (i, 0, 0)),
        compiler_params=params(ROOMY),
        cost_estimate=pl.CostEstimate(flops=2500000, bytes_accessed=6500000, transcendentals=0),
        name="split_weights",
    )(weight)


def margin_kernel(
    groups, rows, slots, gain_row, unroll,
    slot_ref, block_ref, count_ref, weight_a, weight_b, got_ref, surface_ref, coef_ref, mask_ref, land_ref,
    reply_ref, flux_ref,
    weight_ref, value_ref, cell_ref, two_ref, back_ref, stack_ref, sem,
):
    margins = weight_ref.shape[0]
    chunks = sem.shape[0]
    size = margins // chunks
    half = weight_a.shape[0] // size

    def fetch(c):
        source = weight_a if c < half else weight_b
        return pltpu.make_async_copy(
            source.at[pl.ds((c if c < half else c - half) * size, size)], weight_ref.at[pl.ds(c * size, size)], sem.at[c]
        )

    for c in range(chunks):
        fetch(c).start()
    tall = groups * rows
    top = round_up(tall, 2 * ROWS)
    columns = weight_ref.shape[2]
    sources = value_ref.shape[0] // slots
    cells = surface_ref.shape[0]
    count = count_ref[0]
    for a in range(sources):
        for p in range(slots):
            for g in range(groups):
                stack_ref[a * slots + p, g * rows:(g + 1) * rows, :] = (
                    got_ref[pl.ds((a * groups + g) * rows * slots + p, rows, stride=slots), :]
                )
    for s in range(sources * slots):
        value_ref[s] = split(stack_ref[s])
    cell_ref[...] = jnp.zeros_like(cell_ref)
    back_ref[...] = jnp.zeros_like(back_ref)

    for c in range(chunks):
        fetch(c).wait()

        @pl.loop(0, size // unroll)
        def _(step):
            for u in range(unroll):
                k = c * size + step * unroll + u
                target = jnp.where(k < count, block_ref[k], cells)
                one = lax.dot_general(
                    value_ref[slot_ref[k]], weight_ref[k, :columns], (((1,), (1,)), ((), ())),
                    preferred_element_type=F32,
                )
                two = lax.dot_general(
                    value_ref[slot_ref[k], :top], weight_ref[k, columns:], (((1,), (1,)), ((), ())),
                    preferred_element_type=F32,
                )
                cell_ref[target] += one[:tall] + (one[tall:] + two[:tall])

    for j in range(cells):
        cell = cell_ref[j]
        coef = coef_ref[j:j + 1, :]
        land = mask_ref[j:j + 1, :].astype(F32) * land_ref[j:j + 1, :]
        scale = coef / (1.0 + coef * (cell[gain_row:gain_row + 1, :] + land))
        flux = scale * (surface_ref[j] - cell)
        flux_ref[j] = flux
        two_ref[j] = split(flux)

    @pl.loop(0, margins // unroll)
    def _(step):
        for u in range(unroll):
            k = step * unroll + u
            target = jnp.where(k < count, slot_ref[k], sources * slots)
            one = jnp.dot(two_ref[block_ref[k]], weight_ref[k, :columns], preferred_element_type=F32)
            two = jnp.dot(
                two_ref[block_ref[k], :top], weight_ref[k, columns:], preferred_element_type=F32
            )
            back_ref[target] += one[:tall] + (one[tall:] + two[:tall])

    for a in range(sources):
        for p in range(slots):
            for g in range(groups):
                reply_ref[pl.ds((a * groups + g) * rows * slots + p, rows, stride=slots), :] = (
                    back_ref[a * slots + p, g * rows:(g + 1) * rows, :]
                )


def margins_stage(slot, block, count, weights_a, weights_b, got, surface, coef, mask, land,
                  groups, rows, slots, gain_row):
    part, twice, columns = weights_a.shape
    margins = part + weights_b.shape[0]
    width = got.shape[1]
    owners = got.shape[0] // (rows * slots)
    cells, tall, _ = surface.shape
    sources = owners // groups
    chunks = 6
    unroll = math.gcd(16, margins // chunks)
    return pl.pallas_call(
        functools.partial(margin_kernel, groups, rows, slots, gain_row, unroll),
        out_shape=(
            jax.ShapeDtypeStruct(got.shape, F32),
            jax.ShapeDtypeStruct(surface.shape, F32),
        ),
        in_specs=[smem()] * 3 + [hbm()] * 2 + [vmem()] * 5,
        out_specs=(vmem(), vmem()),
        scratch_shapes=[
            pltpu.VMEM((margins, twice, columns), BF16),
            pltpu.VMEM((sources * slots, 2 * tall, width), BF16),
            pltpu.VMEM((cells + 1, tall, width), F32),
            pltpu.VMEM((cells, 2 * tall, width), BF16),
            pltpu.VMEM((sources * slots + 1, tall, width), F32),
            pltpu.VMEM((sources * slots, tall, width), F32),
            pltpu.SemaphoreType.DMA((chunks,)),
        ],
        compiler_params=params(ROOMY),
        cost_estimate=pl.CostEstimate(flops=800000000, bytes_accessed=8000000, transcendentals=0),
        name="margins",
    )(slot, block, count, weights_a, weights_b, got, surface, coef, mask, land)


def unfold_kernel(groups, own, *refs):
    firsts, seconds, after_ref, factor_ref, gain_ref = (
        refs[:groups], refs[groups:2 * groups], *refs[2 * groups:]
    )
    levels = factor_ref.shape[0] // 3
    for q in range(groups):
        factor_ref[:levels, q * own:(q + 1) * own, :] = firsts[q][:levels]
        factor_ref[2 * levels:, q * own:(q + 1) * own, :] = seconds[q][...]
        gain_ref[q * own:(q + 1) * own, :] = firsts[q][levels]
    above = factor_ref[2 * levels]
    inverse = 1.0 - above
    factor_ref[levels] = inverse
    for k in range(1, levels):
        carry = factor_ref[2 * levels + k]
        inverse = (1.0 - carry) * inverse / (inverse + factor_ref[k] * (1.0 - above))
        factor_ref[levels + k] = inverse
        above = carry


def unfold(firsts, seconds, after):
    levels, own, width = seconds[0].shape
    groups = len(seconds)
    blocks = groups * own
    return pl.pallas_call(
        functools.partial(unfold_kernel, groups, own),
        out_shape=(
            jax.ShapeDtypeStruct((3 * levels, blocks, width), F32),
            jax.ShapeDtypeStruct((blocks, width), F32),
        ),
        in_specs=[vmem()] * (2 * groups) + [hbm()],
        out_specs=(vmem(), vmem()),
        compiler_params=params(ROOMY),
        cost_estimate=pl.CostEstimate(flops=1000000, bytes_accessed=3000000, transcendentals=100000),
        name="unfold",
    )(*firsts, *seconds, after)


def finish_kernel(groups, own, rows, slots, me_ref, place_ref, answer_ref, factor_ref, gain_ref,
                  fields_ref, out_ref, held_ref, flux_ref, sem, out_sem):
    me = me_ref[0]
    fetch_fields(me, groups, own, fields_ref, held_ref, sem)
    shares, levels, blocks, _ = held_ref.shape
    flux_ref[...] = jnp.zeros_like(flux_ref)
    pitch = round_up(rows, ROWS)
    for d in range(answer_ref.shape[0] // (rows * slots)):
        for p in range(slots):
            start = pl.multiple_of(place_ref[d * slots + p] * pitch, pitch)
            flux_ref[pl.ds(start, rows), :] += (
                answer_ref[pl.ds(d * rows * slots + p, rows, stride=slots), :]
            )
    for piece, (low, high) in enumerate(bundles(shares)):
        wait_piece(held_ref, sem, piece)
        span = range(low, high)
        state = {f: held_ref[f, 0] for f in span}
        for k in range(1, levels):
            ratio = factor_ref[k]
            for f in span:
                state[f] = held_ref[f, k] + ratio * state[f]
                if k < levels - 1:
                    held_ref[f, k] = state[f]
        inverse = factor_ref[2 * levels - 1]
        for f in span:
            flux = flux_ref[pl.ds(f, blocks, stride=pitch), :]
            state[f] = inverse * state[f] + gain_ref[...] * flux
            held_ref[f, levels - 1] = state[f]
        for k in range(levels - 2, -1, -1):
            inverse, carry = factor_ref[levels + k], factor_ref[2 * levels + k]
            for f in span:
                state[f] = inverse * held_ref[f, k] + carry * state[f]
                held_ref[f, k] = state[f]
        for copy in field_copies(me, groups, own, out_ref, held_ref, out_sem, piece, True):
            copy.start()
    for piece in range(len(bundles(shares))):
        wait_piece(held_ref, out_sem, piece)


def finish(me, place, answer, factor, gain, fields, groups, rows, slots):
    blocks, shares, levels, width = fields.shape
    return pl.pallas_call(
        functools.partial(finish_kernel, groups, blocks // groups, rows, slots),
        out_shape=jax.ShapeDtypeStruct((blocks, shares, levels, width), F32),
        in_specs=[smem(), smem(), vmem(), vmem(), vmem(), hbm()],
        out_specs=hbm(),
        scratch_shapes=[
            pltpu.VMEM((shares, levels, blocks, width), F32),
            pltpu.VMEM(((blocks + 1) * round_up(rows, ROWS), width), F32),
            pltpu.SemaphoreType.DMA((len(bundles(shares)),)),
            pltpu.SemaphoreType.DMA((len(bundles(shares)),)),
        ],
        compiler_params=params(ROOMY),
        cost_estimate=pl.CostEstimate(flops=8000000, bytes_accessed=12000000, transcendentals=0),
        name="finish",
    )(me, place, answer, factor, gain, fields)


def per_device(
    fields_now, upper, lower, surface_gain, route, margin_slot, margin_block, margin_count,
    margin_weight, surface_value, exchange_coef, land_mask, land_gain,
):
    groups = lax.axis_size("xg")
    me = lax.axis_index("xg").astype(jnp.int32)
    blocks, _, shares, width = fields_now.shape
    own = blocks // groups
    rows = shares + 1
    owners, slots = route.shape[1:]
    cells = surface_value.shape[0]

    def shift(array, by):
        return lax.ppermute(array, "xg", [(i, (i + by) % groups) for i in range(groups)])

    def shared(array):
        return [array] + [shift(array, by) for by in range(1, groups)]

    def exchange(array):
        array = array.reshape(owners, rows, slots, width)
        array = lax.all_to_all(array, ("atm", "xg"), split_axis=0, concat_axis=0, tiled=True)
        return array.reshape(owners * rows * slots, width)

    fields = fields_now.transpose(0, 2, 1, 3)
    first, second = factors(upper, lower, surface_gain)
    firsts = shared(first)
    relayed = second
    seconds = [second] + [None] * (groups - 1)
    for by in range(groups - 1, 0, -1):
        relayed = shift(relayed, groups - 1)
        seconds[by] = relayed
    routing = route[0].reshape(owners * slots)
    place = jnp.where(
        routing < blocks,
        lax.rem(me - routing // own + groups, groups) * own + routing % own,
        blocks,
    ).astype(jnp.int32)
    me = me[None]
    weights_a = split_weights(margin_weight[0], 0, margin_weight.shape[1] // 3)
    weights_b = split_weights(margin_weight[0], margin_weight.shape[1] // 3, margin_weight.shape[1])
    surface = jnp.pad(
        surface_value.reshape(cells, groups, shares, width),
        ((0, 0), (0, 0), (0, rows - shares), (0, 0)),
    ).reshape(cells, groups * rows, width)
    send = bottoms(me, place, firsts, fields, owners, slots, rows)
    got = exchange(send)
    reply, flux = margins_stage(
        margin_slot[0], margin_block[0], margin_count, weights_a, weights_b, got, surface,
        exchange_coef, land_mask, land_gain, groups, rows, slots, shares,
    )
    answer = exchange(reply)
    surface_flux = flux.reshape(cells, groups, rows, width)[:, :, :shares].reshape(
        cells, groups * shares, width
    )
    factor, gain = unfold(firsts, seconds, reply)
    out = finish(me, place, answer, factor, gain, fields, groups, rows, slots)
    return out.transpose(0, 2, 1, 3), surface_flux


def solution(mesh):
    in_specs = (
        P("atm", None, "xg", None),
        P(("atm", "xg"), None, None),
        P(("atm", "xg"), None, None),
        P(("atm", "xg"), None),
        P("atm", None, None),
        P(("atm", "xg"), None),
        P(("atm", "xg"), None),
        P(("atm", "xg")),
        P(("atm", "xg"), None, None, None),
        P(("atm", "xg"), None, None),
        P(("atm", "xg"), None),
        P(("atm", "xg"), None),
        P(("atm", "xg"), None),
    )
    out_specs = (P("atm", None, "xg", None), P(("atm", "xg"), None, None))
    return jax.shard_map(
        per_device, mesh=mesh, in_specs=in_specs, out_specs=out_specs, check_vma=False
    )
```

```python
import functools
import math

import jax
import jax.numpy as jnp
from jax import lax
from jax.experimental import pallas as pl
from jax.experimental.pallas import tpu as pltpu
from jax.sharding import PartitionSpec as P

F32 = jnp.float32
BF16 = jnp.bfloat16
ROWS = 8
PIECES = 5
MOST = 67043328
ROOMY = 50 << 20


def vmem():
    return pl.BlockSpec(memory_space=pltpu.VMEM)


def smem():
    return pl.BlockSpec(memory_space=pltpu.SMEM)


def hbm():
    return pl.BlockSpec(memory_space=pltpu.HBM)


def params(limit):
    return pltpu.CompilerParams(vmem_limit_bytes=limit)


def round_up(value, step):
    return -(-value // step) * step


def split(value):
    high = value.astype(BF16).astype(F32)
    return jnp.concatenate([high, value - high], 0).astype(BF16)


def factor_kernel(levels, own, upper_hbm, lower_hbm, gain_hbm, first_ref, second_ref,
                  upper_ref, lower_ref, gain_ref, sem):
    copies = [
        pltpu.make_async_copy(source, target, sem.at[i])
        for i, (source, target) in enumerate(
            ((upper_hbm, upper_ref), (lower_hbm, lower_ref), (gain_hbm, gain_ref))
        )
    ]
    for copy in copies:
        copy.start()
    for copy in copies:
        copy.wait()
    carried = jnp.zeros(gain_ref.shape, F32)
    inverse = carried
    for k in range(levels):
        from_above = upper_ref[pl.ds(k, own, stride=levels), :] if k > 0 else jnp.zeros_like(carried)
        from_below = lower_ref[pl.ds(k, own, stride=levels), :] if k < levels - 1 else jnp.zeros_like(carried)
        if k > 0:
            first_ref[k] = from_above * inverse
        inverse = 1.0 / (1.0 + from_above + from_below - from_above * carried)
        carried = from_below * inverse
        second_ref[k] = carried
    first_ref[0] = inverse
    first_ref[levels] = gain_ref[...] * inverse


def factors(upper, lower, surface_gain):
    own, levels, width = upper.shape
    return pl.pallas_call(
        functools.partial(factor_kernel, levels, own),
        out_shape=(
            jax.ShapeDtypeStruct((levels + 1, own, width), F32),
            jax.ShapeDtypeStruct((levels, own, width), F32),
        ),
        in_specs=[hbm()] * 3,
        out_specs=(vmem(), vmem()),
        scratch_shapes=[
            pltpu.VMEM((own * levels, width), F32),
            pltpu.VMEM((own * levels, width), F32),
            pltpu.VMEM((own, width), F32),
            pltpu.SemaphoreType.DMA((3,)),
        ],
        compiler_params=params(MOST),
        cost_estimate=pl.CostEstimate(flops=1000000, bytes_accessed=400000, transcendentals=30000),
        name="factors",
    )(upper.reshape(own * levels, width), lower.reshape(own * levels, width), surface_gain)


def bundles(shares):
    pieces = min(PIECES, shares)
    edges = [i * shares // pieces for i in range(pieces + 1)]
    return list(zip(edges[:-1], edges[1:]))


def field_copies(me, groups, own, fields_ref, held_ref, sem, piece, out):
    low, high = bundles(held_ref.shape[0])[piece]
    copies = []
    for q in range(groups):
        base = lax.rem(me - q + groups, groups) * own
        for i in range(own):
            far = fields_ref.at[base + i, pl.ds(low, high - low)]
            near = held_ref.at[pl.ds(low, high - low), :, q * own + i, :]
            pair = (near, far) if out else (far, near)
            copies.append(pltpu.make_async_copy(*pair, sem.at[piece]))
    return copies


def fetch_fields(me, groups, own, fields_ref, held_ref, sem):
    for piece in range(len(bundles(held_ref.shape[0]))):
        for copy in field_copies(me, groups, own, fields_ref, held_ref, sem, piece, False):
            copy.start()


def wait_piece(held_ref, sem, piece):
    low, high = bundles(held_ref.shape[0])[piece]
    part = held_ref.at[pl.ds(low, high - low)]
    pltpu.make_async_copy(part, part, sem.at[piece]).wait()


def bottom_kernel(groups, own, rows, slots, me_ref, place_ref, *refs):
    parts, fields_ref, send_ref, held_ref, weight_ref, value_ref, own_ref, sem, own_sem = (
        refs[:groups], *refs[groups:]
    )
    fetch = pltpu.make_async_copy(parts[0], own_ref, own_sem)
    fetch.start()
    fetch_fields(me_ref[0], groups, own, fields_ref, held_ref, sem)
    blocks = groups * own
    pitch = round_up(rows, ROWS)
    levels = held_ref.shape[1]
    shares = held_ref.shape[0]
    for q in range(1, groups):
        weight_ref[:, q * own:(q + 1) * own, :] = parts[q][...]
    fetch.wait()
    weight_ref[:, :own, :] = own_ref[...]
    weight = weight_ref[0]
    for k in range(levels - 1, -1, -1):
        ratio = weight_ref[k]
        weight_ref[k] = weight
        weight = weight * ratio
    value_ref[...] = jnp.zeros_like(value_ref)
    value_ref[pl.ds(shares, blocks, stride=pitch), :] = weight_ref[levels]
    for piece, (low, high) in enumerate(bundles(shares)):
        wait_piece(held_ref, sem, piece)
        sums = {}
        for k in range(levels):
            weight = weight_ref[k]
            for f in range(low, high):
                term = weight * held_ref[f, k]
                slot = (f, k % 2)
                sums[slot] = sums[slot] + term if slot in sums else term
        for f in range(low, high):
            value_ref[pl.ds(f, blocks, stride=pitch), :] = sums[f, 0] + sums[f, 1]
    for d in range(send_ref.shape[0] // (rows * slots)):
        for p in range(slots):
            start = pl.multiple_of(place_ref[d * slots + p] * pitch, pitch)
            send_ref[pl.ds(d * rows * slots + p, rows, stride=slots), :] = value_ref[pl.ds(start, rows), :]


def bottoms(me, place, parts, fields, owners, slots, rows):
    blocks, shares, levels, width = fields.shape
    groups = len(parts)
    own = blocks // groups
    return pl.pallas_call(
        functools.partial(bottom_kernel, groups, own, rows, slots),
        out_shape=jax.ShapeDtypeStruct((owners * rows * slots, width), F32),
        in_specs=[smem(), smem(), hbm()] + [vmem()] * (groups - 1) + [hbm()],
        out_specs=vmem(),
        scratch_shapes=[
            pltpu.VMEM((shares, levels, blocks, width), F32),
            pltpu.VMEM((levels + 1, blocks, width), F32),
            pltpu.VMEM(((blocks + 1) * round_up(rows, ROWS), width), F32),
            pltpu.VMEM((levels + 1, own, width), F32),
            pltpu.SemaphoreType.DMA((len(bundles(shares)),)),
            pltpu.SemaphoreType.DMA(()),
        ],
        compiler_params=params(ROOMY),
        cost_estimate=pl.CostEstimate(flops=4000000, bytes_accessed=7000000, transcendentals=0),
        name="bottoms",
    )(me, place, *parts, fields)


def split_kernel(weight_ref, out_ref):
    value = weight_ref[...]
    size = weight_ref.shape[1]
    high = value.astype(BF16)
    out_ref[:, :size, :] = high
    out_ref[:, size:, :] = (value - high.astype(F32)).astype(BF16)


def split_weights(weight, start, stop, step=8):
    _, cells, columns = weight.shape
    count = stop - start
    step = math.gcd(step, math.gcd(start, count))
    first = start // step
    return pl.pallas_call(
        split_kernel,
        grid=(count // step,),
        out_shape=jax.ShapeDtypeStruct((count, 2 * cells, columns), BF16),
        in_specs=[pl.BlockSpec((step, cells, columns), lambda i: (first + i, 0, 0))],
        out_specs=pl.BlockSpec((step, 2 * cells, columns), lambda i: (i, 0, 0)),
        compiler_params=params(ROOMY),
        cost_estimate=pl.CostEstimate(flops=2500000, bytes_accessed=6500000, transcendentals=0),
        name="split_weights",
    )(weight)


def margin_kernel(
    groups, rows, slots, gain_row, unroll,
    slot_ref, block_ref, count_ref, weight_a, weight_b, got_ref, surface_ref, coef_ref, mask_ref, land_ref,
    reply_ref, flux_ref,
    weight_ref, value_ref, cell_ref, two_ref, back_ref, stack_ref, sem,
):
    margins = weight_ref.shape[0]
    chunks = sem.shape[0]
    size = margins // chunks
    half = weight_a.shape[0] // size

    def fetch(c):
        source = weight_a if c < half else weight_b
        return pltpu.make_async_copy(
            source.at[pl.ds((c if c < half else c - half) * size, size)], weight_ref.at[pl.ds(c * size, size)], sem.at[c]
        )

    for c in range(chunks):
        fetch(c).start()
    tall = groups * rows
    top = round_up(tall, 2 * ROWS)
    columns = weight_ref.shape[2]
    sources = value_ref.shape[0] // slots
    cells = surface_ref.shape[0]
    count = count_ref[0]
    for a in range(sources):
        for p in range(slots):
            for g in range(groups):
                stack_ref[a * slots + p, g * rows:(g + 1) * rows, :] = (
                    got_ref[pl.ds((a * groups + g) * rows * slots + p, rows, stride=slots), :]
                )
    for s in range(sources * slots):
        value_ref[s] = split(stack_ref[s])
    cell_ref[...] = jnp.zeros_like(cell_ref)
    back_ref[...] = jnp.zeros_like(back_ref)

    for c in range(chunks):
        fetch(c).wait()

        @pl.loop(0, size // unroll)
        def _(step):
            for u in range(unroll):
                k = c * size + step * unroll + u
                target = jnp.where(k < count, block_ref[k], cells)
                one = lax.dot_general(
                    value_ref[slot_ref[k]], weight_ref[k, :columns], (((1,), (1,)), ((), ())),
                    preferred_element_type=F32,
                )
                two = lax.dot_general(
                    value_ref[slot_ref[k], :top], weight_ref[k, columns:], (((1,), (1,)), ((), ())),
                    preferred_element_type=F32,
                )
                cell_ref[target] += one[:tall] + (one[tall:] + two[:tall])

    for j in range(cells):
        cell = cell_ref[j]
        coef = coef_ref[j:j + 1, :]
        land = mask_ref[j:j + 1, :].astype(F32) * land_ref[j:j + 1, :]
        scale = coef / (1.0 + coef * (cell[gain_row:gain_row + 1, :] + land))
        flux = scale * (surface_ref[j] - cell)
        flux_ref[j] = flux
        two_ref[j] = split(flux)

    @pl.loop(0, margins // unroll)
    def _(step):
        for u in range(unroll):
            k = step * unroll + u
            target = jnp.where(k < count, slot_ref[k], sources * slots)
            one = jnp.dot(two_ref[block_ref[k]], weight_ref[k, :columns], preferred_element_type=F32)
            two = jnp.dot(
                two_ref[block_ref[k], :top], weight_ref[k, columns:], preferred_element_type=F32
            )
            back_ref[target] += one[:tall] + (one[tall:] + two[:tall])

    for a in range(sources):
        for p in range(slots):
            for g in range(groups):
                reply_ref[pl.ds((a * groups + g) * rows * slots + p, rows, stride=slots), :] = (
                    back_ref[a * slots + p, g * rows:(g + 1) * rows, :]
                )


def margins_stage(slot, block, count, weights_a, weights_b, got, surface, coef, mask, land,
                  groups, rows, slots, gain_row):
    part, twice, columns = weights_a.shape
    margins = part + weights_b.shape[0]
    width = got.shape[1]
    owners = got.shape[0] // (rows * slots)
    cells, tall, _ = surface.shape
    sources = owners // groups
    chunks = 6
    unroll = math.gcd(16, margins // chunks)
    return pl.pallas_call(
        functools.partial(margin_kernel, groups, rows, slots, gain_row, unroll),
        out_shape=(
            jax.ShapeDtypeStruct(got.shape, F32),
            jax.ShapeDtypeStruct(surface.shape, F32),
        ),
        in_specs=[smem()] * 3 + [hbm()] * 2 + [vmem()] * 5,
        out_specs=(vmem(), vmem()),
        scratch_shapes=[
            pltpu.VMEM((margins, twice, columns), BF16),
            pltpu.VMEM((sources * slots, 2 * tall, width), BF16),
            pltpu.VMEM((cells + 1, tall, width), F32),
            pltpu.VMEM((cells, 2 * tall, width), BF16),
            pltpu.VMEM((sources * slots + 1, tall, width), F32),
            pltpu.VMEM((sources * slots, tall, width), F32),
            pltpu.SemaphoreType.DMA((chunks,)),
        ],
        compiler_params=params(ROOMY),
        cost_estimate=pl.CostEstimate(flops=800000000, bytes_accessed=8000000, transcendentals=0),
        name="margins",
    )(slot, block, count, weights_a, weights_b, got, surface, coef, mask, land)


def unfold(groups, own, firsts, seconds, factor_ref, gain_ref):
    levels = factor_ref.shape[0] // 3
    for q in range(groups):
        factor_ref[:levels, q * own:(q + 1) * own, :] = firsts[q][:levels]
        factor_ref[2 * levels:, q * own:(q + 1) * own, :] = seconds[q][...]
        gain_ref[q * own:(q + 1) * own, :] = firsts[q][levels]
    above = factor_ref[2 * levels]
    inverse = 1.0 - above
    factor_ref[levels] = inverse
    for k in range(1, levels):
        carry = factor_ref[2 * levels + k]
        inverse = (1.0 - carry) * inverse / (inverse + factor_ref[k] * (1.0 - above))
        factor_ref[levels + k] = inverse
        above = carry


def finish_kernel(groups, own, rows, slots, me_ref, place_ref, answer_ref, *refs):
    firsts, seconds, fields_ref, out_ref, held_ref, factor_ref, gain_ref, flux_ref, sem, out_sem = (
        refs[:groups], refs[groups:2 * groups], *refs[2 * groups:]
    )
    me = me_ref[0]
    fetch_fields(me, groups, own, fields_ref, held_ref, sem)
    unfold(groups, own, firsts, seconds, factor_ref, gain_ref)
    shares, levels, blocks, _ = held_ref.shape
    flux_ref[...] = jnp.zeros_like(flux_ref)
    pitch = round_up(rows, ROWS)
    for d in range(answer_ref.shape[0] // (rows * slots)):
        for p in range(slots):
            start = pl.multiple_of(place_ref[d * slots + p] * pitch, pitch)
            flux_ref[pl.ds(start, rows), :] += (
                answer_ref[pl.ds(d * rows * slots + p, rows, stride=slots), :]
            )
    for piece, (low, high) in enumerate(bundles(shares)):
        wait_piece(held_ref, sem, piece)
        span = range(low, high)
        state = {f: held_ref[f, 0] for f in span}
        for k in range(1, levels):
            ratio = factor_ref[k]
            for f in span:
                state[f] = held_ref[f, k] + ratio * state[f]
                if k < levels - 1:
                    held_ref[f, k] = state[f]
        inverse = factor_ref[2 * levels - 1]
        for f in span:
            flux = flux_ref[pl.ds(f, blocks, stride=pitch), :]
            state[f] = inverse * state[f] + gain_ref[...] * flux
            held_ref[f, levels - 1] = state[f]
        for k in range(levels - 2, -1, -1):
            inverse, carry = factor_ref[levels + k], factor_ref[2 * levels + k]
            for f in span:
                state[f] = inverse * held_ref[f, k] + carry * state[f]
                held_ref[f, k] = state[f]
        for copy in field_copies(me, groups, own, out_ref, held_ref, out_sem, piece, True):
            copy.start()
    for piece in range(len(bundles(shares))):
        wait_piece(held_ref, out_sem, piece)


def finish(me, place, answer, firsts, seconds, fields, rows, slots):
    blocks, shares, levels, width = fields.shape
    groups = len(firsts)
    return pl.pallas_call(
        functools.partial(finish_kernel, groups, blocks // groups, rows, slots),
        out_shape=jax.ShapeDtypeStruct((blocks, shares, levels, width), F32),
        in_specs=[smem(), smem(), vmem()] + [vmem()] * (2 * groups) + [hbm()],
        out_specs=hbm(),
        scratch_shapes=[
            pltpu.VMEM((shares, levels, blocks, width), F32),
            pltpu.VMEM((3 * levels, blocks, width), F32),
            pltpu.VMEM((blocks, width), F32),
            pltpu.VMEM(((blocks + 1) * round_up(rows, ROWS), width), F32),
            pltpu.SemaphoreType.DMA((len(bundles(shares)),)),
            pltpu.SemaphoreType.DMA((len(bundles(shares)),)),
        ],
        compiler_params=params(ROOMY),
        cost_estimate=pl.CostEstimate(flops=8000000, bytes_accessed=12000000, transcendentals=0),
        name="finish",
    )(me, place, answer, *firsts, *seconds, fields)


def per_device(
    fields_now, upper, lower, surface_gain, route, margin_slot, margin_block, margin_count,
    margin_weight, surface_value, exchange_coef, land_mask, land_gain,
):
    groups = lax.axis_size("xg")
    me = lax.axis_index("xg").astype(jnp.int32)
    blocks, _, shares, width = fields_now.shape
    own = blocks // groups
    rows = shares + 1
    owners, slots = route.shape[1:]
    cells = surface_value.shape[0]

    def shift(array, by):
        return lax.ppermute(array, "xg", [(i, (i + by) % groups) for i in range(groups)])

    def shared(array):
        return [array] + [shift(array, by) for by in range(1, groups)]

    def exchange(array):
        array = array.reshape(owners, rows, slots, width)
        array = lax.all_to_all(array, ("atm", "xg"), split_axis=0, concat_axis=0, tiled=True)
        return array.reshape(owners * rows * slots, width)

    fields = fields_now.transpose(0, 2, 1, 3)
    first, second = factors(upper, lower, surface_gain)
    firsts = shared(first)
    routing = route[0].reshape(owners * slots)
    place = jnp.where(
        routing < blocks,
        lax.rem(me - routing // own + groups, groups) * own + routing % own,
        blocks,
    ).astype(jnp.int32)
    me = me[None]
    weights_a = split_weights(margin_weight[0], 0, margin_weight.shape[1] // 6)
    weights_b = split_weights(margin_weight[0], margin_weight.shape[1] // 6, margin_weight.shape[1])
    surface = jnp.pad(
        surface_value.reshape(cells, groups, shares, width),
        ((0, 0), (0, 0), (0, rows - shares), (0, 0)),
    ).reshape(cells, groups * rows, width)
    send = bottoms(me, place, firsts, fields, owners, slots, rows)
    got = exchange(send)
    seconds = [second] + [None] * (groups - 1)
    seconds[1], seconds[groups - 1] = shift(second, 1), shift(second, groups - 1)
    for by in range(groups - 2, 1, -1):
        seconds[by] = shift(seconds[by + 1], groups - 1)
    reply, flux = margins_stage(
        margin_slot[0], margin_block[0], margin_count, weights_a, weights_b, got, surface,
        exchange_coef, land_mask, land_gain, groups, rows, slots, shares,
    )
    answer = exchange(reply)
    surface_flux = flux.reshape(cells, groups, rows, width)[:, :, :shares].reshape(
        cells, groups * shares, width
    )
    out = finish(me, place, answer, firsts, seconds, fields, rows, slots)
    return out.transpose(0, 2, 1, 3), surface_flux


def solution(mesh):
    in_specs = (
        P("atm", None, "xg", None),
        P(("atm", "xg"), None, None),
        P(("atm", "xg"), None, None),
        P(("atm", "xg"), None),
        P("atm", None, None),
        P(("atm", "xg"), None),
        P(("atm", "xg"), None),
        P(("atm", "xg")),
        P(("atm", "xg"), None, None, None),
        P(("atm", "xg"), None, None),
        P(("atm", "xg"), None),
        P(("atm", "xg"), None),
        P(("atm", "xg"), None),
    )
    out_specs = (P("atm", None, "xg", None), P(("atm", "xg"), None, None))
    return jax.shard_map(
        per_device, mesh=mesh, in_specs=in_specs, out_specs=out_specs, check_vma=False
    )
```

```python
import functools
import math

import jax
import jax.numpy as jnp
from jax import lax
from jax.experimental import pallas as pl
from jax.experimental.pallas import tpu as pltpu
from jax.sharding import PartitionSpec as P

F32 = jnp.float32
BF16 = jnp.bfloat16
ROWS = 8
PIECES = 5
MOST = 67043328
ROOMY = 50 << 20


def vmem():
    return pl.BlockSpec(memory_space=pltpu.VMEM)


def smem():
    return pl.BlockSpec(memory_space=pltpu.SMEM)


def hbm():
    return pl.BlockSpec(memory_space=pltpu.HBM)


def params(limit):
    return pltpu.CompilerParams(vmem_limit_bytes=limit)


def round_up(value, step):
    return -(-value // step) * step


def split(value):
    tall, width = value.shape
    high = value.astype(BF16).astype(F32)
    gap = jnp.zeros((round_up(tall, 2 * ROWS) - tall, width), F32)
    return jnp.concatenate([high, gap, value - high, gap], 0).astype(BF16)


def factor_kernel(levels, own, upper_hbm, lower_hbm, gain_hbm, first_ref, second_ref,
                  upper_ref, lower_ref, gain_ref, sem):
    copies = [
        pltpu.make_async_copy(source, target, sem.at[i])
        for i, (source, target) in enumerate(
            ((upper_hbm, upper_ref), (lower_hbm, lower_ref), (gain_hbm, gain_ref))
        )
    ]
    for copy in copies:
        copy.start()
    for copy in copies:
        copy.wait()
    carried = jnp.zeros(gain_ref.shape, F32)
    inverse = carried
    for k in range(levels):
        from_above = upper_ref[pl.ds(k, own, stride=levels), :] if k > 0 else jnp.zeros_like(carried)
        from_below = lower_ref[pl.ds(k, own, stride=levels), :] if k < levels - 1 else jnp.zeros_like(carried)
        if k > 0:
            first_ref[k] = from_above * inverse
        inverse = 1.0 / (1.0 + from_above + from_below - from_above * carried)
        carried = from_below * inverse
        second_ref[k] = carried
    first_ref[0] = inverse
    first_ref[levels] = gain_ref[...] * inverse


def factors(upper, lower, surface_gain):
    own, levels, width = upper.shape
    return pl.pallas_call(
        functools.partial(factor_kernel, levels, own),
        out_shape=(
            jax.ShapeDtypeStruct((levels + 1, own, width), F32),
            jax.ShapeDtypeStruct((levels, own, width), F32),
        ),
        in_specs=[hbm()] * 3,
        out_specs=(vmem(), vmem()),
        scratch_shapes=[
            pltpu.VMEM((own * levels, width), F32),
            pltpu.VMEM((own * levels, width), F32),
            pltpu.VMEM((own, width), F32),
            pltpu.SemaphoreType.DMA((3,)),
        ],
        compiler_params=params(MOST),
        cost_estimate=pl.CostEstimate(flops=1000000, bytes_accessed=400000, transcendentals=30000),
        name="factors",
    )(upper.reshape(own * levels, width), lower.reshape(own * levels, width), surface_gain)


def bundles(shares):
    pieces = min(PIECES, shares)
    edges = [i * shares // pieces for i in range(pieces + 1)]
    return list(zip(edges[:-1], edges[1:]))


def field_copies(me, groups, own, fields_ref, held_ref, sem, piece, out):
    low, high = bundles(held_ref.shape[0])[piece]
    copies = []
    for q in range(groups):
        base = lax.rem(me - q + groups, groups) * own
        for i in range(own):
            far = fields_ref.at[base + i, pl.ds(low, high - low)]
            near = held_ref.at[pl.ds(low, high - low), :, q * own + i, :]
            pair = (near, far) if out else (far, near)
            copies.append(pltpu.make_async_copy(*pair, sem.at[piece]))
    return copies


def fetch_fields(me, groups, own, fields_ref, held_ref, sem):
    for piece in range(len(bundles(held_ref.shape[0]))):
        for copy in field_copies(me, groups, own, fields_ref, held_ref, sem, piece, False):
            copy.start()


def wait_piece(held_ref, sem, piece):
    low, high = bundles(held_ref.shape[0])[piece]
    part = held_ref.at[pl.ds(low, high - low)]
    pltpu.make_async_copy(part, part, sem.at[piece]).wait()


def bottom_kernel(groups, own, rows, slots, me_ref, place_ref, *refs):
    parts, fields_ref, send_ref, held_ref, weight_ref, value_ref, own_ref, sem, own_sem = (
        refs[:groups], *refs[groups:]
    )
    fetch = pltpu.make_async_copy(parts[0], own_ref, own_sem)
    fetch.start()
    fetch_fields(me_ref[0], groups, own, fields_ref, held_ref, sem)
    blocks = groups * own
    pitch = round_up(rows, ROWS)
    levels = held_ref.shape[1]
    shares = held_ref.shape[0]
    for q in range(1, groups):
        weight_ref[:, q * own:(q + 1) * own, :] = parts[q][...]
    fetch.wait()
    weight_ref[:, :own, :] = own_ref[...]
    weight = weight_ref[0]
    for k in range(levels - 1, -1, -1):
        ratio = weight_ref[k]
        weight_ref[k] = weight
        weight = weight * ratio
    value_ref[...] = jnp.zeros_like(value_ref)
    value_ref[pl.ds(shares, blocks, stride=pitch), :] = weight_ref[levels]
    for piece, (low, high) in enumerate(bundles(shares)):
        wait_piece(held_ref, sem, piece)
        sums = {}
        for k in range(levels):
            weight = weight_ref[k]
            for f in range(low, high):
                term = weight * held_ref[f, k]
                slot = (f, k % 2)
                sums[slot] = sums[slot] + term if slot in sums else term
        for f in range(low, high):
            value_ref[pl.ds(f, blocks, stride=pitch), :] = sums[f, 0] + sums[f, 1]
    for d in range(send_ref.shape[0] // (rows * slots)):
        for p in range(slots):
            start = pl.multiple_of(place_ref[d * slots + p] * pitch, pitch)
            send_ref[pl.ds(d * rows * slots + p, rows, stride=slots), :] = value_ref[pl.ds(start, rows), :]


def bottoms(me, place, parts, fields, owners, slots, rows):
    blocks, shares, levels, width = fields.shape
    groups = len(parts)
    own = blocks // groups
    return pl.pallas_call(
        functools.partial(bottom_kernel, groups, own, rows, slots),
        out_shape=jax.ShapeDtypeStruct((owners * rows * slots, width), F32),
        in_specs=[smem(), smem(), hbm()] + [vmem()] * (groups - 1) + [hbm()],
        out_specs=vmem(),
        scratch_shapes=[
            pltpu.VMEM((shares, levels, blocks, width), F32),
            pltpu.VMEM((levels + 1, blocks, width), F32),
            pltpu.VMEM(((blocks + 1) * round_up(rows, ROWS), width), F32),
            pltpu.VMEM((levels + 1, own, width), F32),
            pltpu.SemaphoreType.DMA((len(bundles(shares)),)),
            pltpu.SemaphoreType.DMA(()),
        ],
        compiler_params=params(ROOMY),
        cost_estimate=pl.CostEstimate(flops=4000000, bytes_accessed=7000000, transcendentals=0),
        name="bottoms",
    )(me, place, *parts, fields)


def split_kernel(weight_ref, out_ref):
    value = weight_ref[...]
    size = weight_ref.shape[1]
    high = value.astype(BF16)
    out_ref[:, :size, :] = high
    out_ref[:, size:, :] = (value - high.astype(F32)).astype(BF16)


def split_weights(weight, start, stop, step=8):
    _, cells, columns = weight.shape
    count = stop - start
    step = math.gcd(step, math.gcd(start, count))
    first = start // step
    return pl.pallas_call(
        split_kernel,
        grid=(count // step,),
        out_shape=jax.ShapeDtypeStruct((count, 2 * cells, columns), BF16),
        in_specs=[pl.BlockSpec((step, cells, columns), lambda i: (first + i, 0, 0))],
        out_specs=pl.BlockSpec((step, 2 * cells, columns), lambda i: (i, 0, 0)),
        compiler_params=params(ROOMY),
        cost_estimate=pl.CostEstimate(flops=2500000, bytes_accessed=6500000, transcendentals=0),
        name="split_weights",
    )(weight)


def margin_kernel(
    groups, rows, slots, gain_row, unroll,
    slot_ref, block_ref, count_ref, weight_a, weight_b, got_ref, surface_ref, coef_ref, mask_ref, land_ref,
    reply_ref, flux_ref,
    weight_ref, value_ref, cell_ref, two_ref, back_ref, stack_ref, sem,
):
    margins = weight_ref.shape[0]
    chunks = sem.shape[0]
    size = margins // chunks
    half = weight_a.shape[0] // size

    def fetch(c):
        source = weight_a if c < half else weight_b
        return pltpu.make_async_copy(
            source.at[pl.ds((c if c < half else c - half) * size, size)], weight_ref.at[pl.ds(c * size, size)], sem.at[c]
        )

    for c in range(chunks):
        fetch(c).start()
    tall = groups * rows
    top = round_up(tall, 2 * ROWS)
    columns = weight_ref.shape[2]
    sources = value_ref.shape[0] // slots
    cells = surface_ref.shape[0]
    count = count_ref[0]
    for a in range(sources):
        for p in range(slots):
            for g in range(groups):
                stack_ref[a * slots + p, g * rows:(g + 1) * rows, :] = (
                    got_ref[pl.ds((a * groups + g) * rows * slots + p, rows, stride=slots), :]
                )
    for s in range(sources * slots):
        value_ref[s] = split(stack_ref[s])
    cell_ref[...] = jnp.zeros_like(cell_ref)
    back_ref[...] = jnp.zeros_like(back_ref)

    for c in range(chunks):
        fetch(c).wait()

        @pl.loop(0, size // unroll)
        def _(step):
            for u in range(unroll):
                k = c * size + step * unroll + u
                target = jnp.where(k < count, block_ref[k], cells)
                one = lax.dot_general(
                    value_ref[slot_ref[k]], weight_ref[k, :columns], (((1,), (1,)), ((), ())),
                    preferred_element_type=F32,
                )
                two = lax.dot_general(
                    value_ref[slot_ref[k], :top], weight_ref[k, columns:], (((1,), (1,)), ((), ())),
                    preferred_element_type=F32,
                )
                cell_ref[target] += one[:tall] + (one[top:top + tall] + two[:tall])

    for j in range(cells):
        cell = cell_ref[j]
        coef = coef_ref[j:j + 1, :]
        land = mask_ref[j:j + 1, :].astype(F32) * land_ref[j:j + 1, :]
        scale = coef / (1.0 + coef * (cell[gain_row:gain_row + 1, :] + land))
        flux = scale * (surface_ref[j] - cell)
        flux_ref[j] = flux
        two_ref[j] = split(flux)

    @pl.loop(0, margins // unroll)
    def _(step):
        for u in range(unroll):
            k = step * unroll + u
            target = jnp.where(k < count, slot_ref[k], sources * slots)
            one = jnp.dot(two_ref[block_ref[k]], weight_ref[k, :columns], preferred_element_type=F32)
            two = jnp.dot(
                two_ref[block_ref[k], :top], weight_ref[k, columns:], preferred_element_type=F32
            )
            back_ref[target] += one[:tall] + (one[top:top + tall] + two[:tall])

    for a in range(sources):
        for p in range(slots):
            for g in range(groups):
                reply_ref[pl.ds((a * groups + g) * rows * slots + p, rows, stride=slots), :] = (
                    back_ref[a * slots + p, g * rows:(g + 1) * rows, :]
                )


def margins_stage(slot, block, count, weights_a, weights_b, got, surface, coef, mask, land,
                  groups, rows, slots, gain_row):
    part, twice, columns = weights_a.shape
    margins = part + weights_b.shape[0]
    width = got.shape[1]
    owners = got.shape[0] // (rows * slots)
    cells, tall, _ = surface.shape
    sources = owners // groups
    chunks = 6
    unroll = math.gcd(16, margins // chunks)
    return pl.pallas_call(
        functools.partial(margin_kernel, groups, rows, slots, gain_row, unroll),
        out_shape=(
            jax.ShapeDtypeStruct(got.shape, F32),
            jax.ShapeDtypeStruct(surface.shape, F32),
        ),
        in_specs=[smem()] * 3 + [hbm()] * 2 + [vmem()] * 5,
        out_specs=(vmem(), vmem()),
        scratch_shapes=[
            pltpu.VMEM((margins, twice, columns), BF16),
            pltpu.VMEM((sources * slots, 2 * round_up(tall, 2 * ROWS), width), BF16),
            pltpu.VMEM((cells + 1, tall, width), F32),
            pltpu.VMEM((cells, 2 * round_up(tall, 2 * ROWS), width), BF16),
            pltpu.VMEM((sources * slots + 1, tall, width), F32),
            pltpu.VMEM((sources * slots, tall, width), F32),
            pltpu.SemaphoreType.DMA((chunks,)),
        ],
        compiler_params=params(ROOMY),
        cost_estimate=pl.CostEstimate(flops=800000000, bytes_accessed=8000000, transcendentals=0),
        name="margins",
    )(slot, block, count, weights_a, weights_b, got, surface, coef, mask, land)


def unfold(groups, own, firsts, seconds, factor_ref, gain_ref):
    levels = factor_ref.shape[0] // 3
    for q in range(groups):
        factor_ref[:levels, q * own:(q + 1) * own, :] = firsts[q][:levels]
        factor_ref[2 * levels:, q * own:(q + 1) * own, :] = seconds[q][...]
        gain_ref[q * own:(q + 1) * own, :] = firsts[q][levels]
    above = factor_ref[2 * levels]
    inverse = 1.0 - above
    factor_ref[levels] = inverse
    for k in range(1, levels):
        carry = factor_ref[2 * levels + k]
        inverse = (1.0 - carry) * inverse / (inverse + factor_ref[k] * (1.0 - above))
        factor_ref[levels + k] = inverse
        above = carry


def finish_kernel(groups, own, rows, slots, me_ref, place_ref, answer_ref, *refs):
    firsts, seconds, fields_ref, out_ref, held_ref, factor_ref, gain_ref, flux_ref, sem, out_sem = (
        refs[:groups], refs[groups:2 * groups], *refs[2 * groups:]
    )
    me = me_ref[0]
    fetch_fields(me, groups, own, fields_ref, held_ref, sem)
    unfold(groups, own, firsts, seconds, factor_ref, gain_ref)
    shares, levels, blocks, _ = held_ref.shape
    flux_ref[...] = jnp.zeros_like(flux_ref)
    pitch = round_up(rows, ROWS)
    for d in range(answer_ref.shape[0] // (rows * slots)):
        for p in range(slots):
            start = pl.multiple_of(place_ref[d * slots + p] * pitch, pitch)
            flux_ref[pl.ds(start, rows), :] += (
                answer_ref[pl.ds(d * rows * slots + p, rows, stride=slots), :]
            )
    for piece, (low, high) in enumerate(bundles(shares)):
        wait_piece(held_ref, sem, piece)
        span = range(low, high)
        state = {f: held_ref[f, 0] for f in span}
        for k in range(1, levels):
            ratio = factor_ref[k]
            for f in span:
                state[f] = held_ref[f, k] + ratio * state[f]
                if k < levels - 1:
                    held_ref[f, k] = state[f]
        inverse = factor_ref[2 * levels - 1]
        for f in span:
            flux = flux_ref[pl.ds(f, blocks, stride=pitch), :]
            state[f] = inverse * state[f] + gain_ref[...] * flux
            held_ref[f, levels - 1] = state[f]
        for k in range(levels - 2, -1, -1):
            inverse, carry = factor_ref[levels + k], factor_ref[2 * levels + k]
            for f in span:
                state[f] = inverse * held_ref[f, k] + carry * state[f]
                held_ref[f, k] = state[f]
        for copy in field_copies(me, groups, own, out_ref, held_ref, out_sem, piece, True):
            copy.start()
    for piece in range(len(bundles(shares))):
        wait_piece(held_ref, out_sem, piece)


def finish(me, place, answer, firsts, seconds, fields, rows, slots):
    blocks, shares, levels, width = fields.shape
    groups = len(firsts)
    return pl.pallas_call(
        functools.partial(finish_kernel, groups, blocks // groups, rows, slots),
        out_shape=jax.ShapeDtypeStruct((blocks, shares, levels, width), F32),
        in_specs=[smem(), smem(), vmem()] + [vmem()] * (2 * groups) + [hbm()],
        out_specs=hbm(),
        scratch_shapes=[
            pltpu.VMEM((shares, levels, blocks, width), F32),
            pltpu.VMEM((3 * levels, blocks, width), F32),
            pltpu.VMEM((blocks, width), F32),
            pltpu.VMEM(((blocks + 1) * round_up(rows, ROWS), width), F32),
            pltpu.SemaphoreType.DMA((len(bundles(shares)),)),
            pltpu.SemaphoreType.DMA((len(bundles(shares)),)),
        ],
        compiler_params=params(ROOMY),
        cost_estimate=pl.CostEstimate(flops=8000000, bytes_accessed=12000000, transcendentals=0),
        name="finish",
    )(me, place, answer, *firsts, *seconds, fields)


def per_device(
    fields_now, upper, lower, surface_gain, route, margin_slot, margin_block, margin_count,
    margin_weight, surface_value, exchange_coef, land_mask, land_gain,
):
    groups = lax.axis_size("xg")
    me = lax.axis_index("xg").astype(jnp.int32)
    blocks, _, shares, width = fields_now.shape
    own = blocks // groups
    rows = shares + 1
    owners, slots = route.shape[1:]
    cells = surface_value.shape[0]

    def shift(array, by):
        return lax.ppermute(array, "xg", [(i, (i + by) % groups) for i in range(groups)])

    def shared(array):
        return [array] + [shift(array, by) for by in range(1, groups)]

    def exchange(array):
        array = array.reshape(owners, rows, slots, width)
        array = lax.all_to_all(array, ("atm", "xg"), split_axis=0, concat_axis=0, tiled=True)
        return array.reshape(owners * rows * slots, width)

    fields = fields_now.transpose(0, 2, 1, 3)
    first, second = factors(upper, lower, surface_gain)
    firsts = shared(first)
    routing = route[0].reshape(owners * slots)
    place = jnp.where(
        routing < blocks,
        lax.rem(me - routing // own + groups, groups) * own + routing % own,
        blocks,
    ).astype(jnp.int32)
    me = me[None]
    weights_a = split_weights(margin_weight[0], 0, margin_weight.shape[1] // 6)
    weights_b = split_weights(margin_weight[0], margin_weight.shape[1] // 6, margin_weight.shape[1])
    surface = jnp.pad(
        surface_value.reshape(cells, groups, shares, width),
        ((0, 0), (0, 0), (0, rows - shares), (0, 0)),
    ).reshape(cells, groups * rows, width)
    send = bottoms(me, place, firsts, fields, owners, slots, rows)
    got = exchange(send)
    seconds = [second] + [None] * (groups - 1)
    seconds[1], seconds[groups - 1] = shift(second, 1), shift(second, groups - 1)
    for by in range(groups - 2, 1, -1):
        seconds[by] = shift(seconds[by + 1], groups - 1)
    reply, flux = margins_stage(
        margin_slot[0], margin_block[0], margin_count, weights_a, weights_b, got, surface,
        exchange_coef, land_mask, land_gain, groups, rows, slots, shares,
    )
    answer = exchange(reply)
    surface_flux = flux.reshape(cells, groups, rows, width)[:, :, :shares].reshape(
        cells, groups * shares, width
    )
    out = finish(me, place, answer, firsts, seconds, fields, rows, slots)
    return out.transpose(0, 2, 1, 3), surface_flux


def solution(mesh):
    in_specs = (
        P("atm", None, "xg", None),
        P(("atm", "xg"), None, None),
        P(("atm", "xg"), None, None),
        P(("atm", "xg"), None),
        P("atm", None, None),
        P(("atm", "xg"), None),
        P(("atm", "xg"), None),
        P(("atm", "xg")),
        P(("atm", "xg"), None, None, None),
        P(("atm", "xg"), None, None),
        P(("atm", "xg"), None),
        P(("atm", "xg"), None),
        P(("atm", "xg"), None),
    )
    out_specs = (P("atm", None, "xg", None), P(("atm", "xg"), None, None))
    return jax.shard_map(
        per_device, mesh=mesh, in_specs=in_specs, out_specs=out_specs, check_vma=False
    )
```
